32 devices in a mesh: gx: 4 (over y, x), gz: 8 (over z, core).
Axes of the slice: x: 2, y: 2, z: 4, core: 2. Of those that a mesh axis runs over, the one named last changes fastest.
Arguments:
- high_u: bfloat16 [128, 256, 512], P('gx', 'gz'), may hold values from -6 to 6
- high_v: bfloat16 [128, 256, 512], P('gx', 'gz'), may hold values from -6 to 6
- low_u: bfloat16 [512, 512], P(('gx', 'gz')), may hold values from -0.5 to 0.5
- low_v: bfloat16 [512, 512], P(('gx', 'gz')), may hold values from -0.5 to 0.5
- low_kx: int32 [512], P(('gx', 'gz')), may hold values from 0 to 64, as said below
- low_kz: int32 [512], P(('gx', 'gz')), may hold values from 0 to 64, as said below
- tau_inverse: bfloat16 [512, 512, 512], P(('gx', 'gz')), may hold values from -0.25 to 0.25
Outputs:
- high_term: bfloat16 [128, 256, 512], P('gx', 'gz')
- low_response: float32 [512, 512], P(('gx', 'gz'))
The draws below stay inside these ranges and needn't reach their ends.
Inputs may be any that keep to these rules, and one draw needn't show every extreme that they name: Slot m holds the retained mode (low_kx[m], low_kz[m]); no two slots hold the same pair; the device that holds slot m owns that mode. `low_kz`: paired with low_kx slot by slot.
All inputs are finite; a program needn't handle non-finite values.
Results may differ from the reference program's by a relative error of at most 0.0047.
Values may be sent and summed in bfloat16 or wider, within the bound.
A program may use at most 128 MiB of HBM per device.

```python
import math
import jax
import jax.numpy as jnp
from jax import lax

NY = 512
KL = 32
LOW_DEV = 16
CX = 32
NX = 128
NZ = 256
LOW_MODES = 512


def mode_pairs(key):
    side = 2 * KL + 1
    order = jax.random.permutation(jax.random.fold_in(key, 7), side * side)[:LOW_MODES]
    return ((order // side).astype(jnp.int32), (order % side).astype(jnp.int32))


def draw_low_kx(key, part):
    return mode_pairs(key)[0]


def draw_low_kz(key, part):
    return mode_pairs(key)[1]


def steps_of(own_key, dims, split, least, high):
    gain = 1.0
    for dim, parts in split:
        steps = jax.random.uniform(jax.random.fold_in(jax.random.fold_in(own_key, 6), dim), (parts,), jnp.float32, least / len(split), high / len(split))
        gain = gain * jnp.repeat(jnp.exp(steps), dims[dim] // parts).reshape((-1,) + (1,) * (len(dims) - 1 - dim))
    return gain


def centred(key, dims, deviation, bound, cuts=(), kind=jnp.bfloat16):
    entries = jax.random.normal(key, dims, jnp.float32) * deviation
    if len(cuts) > 0:
        entries = steps_of(key, dims, cuts, -0.22, 0.18) * entries
    return jnp.clip(entries, min=-bound, max=bound).astype(kind)


def setup_inputs(seed: int = 0) -> dict:
    seeds = jax.random.split(jax.random.key(seed), 8)
    return {
        "high_u": centred(seeds[0], (NX, NZ, NY), 1.0, 6.0, ((0, 4), (1, 8))),
        "high_v": centred(seeds[1], (NX, NZ, NY), 1.0, 6.0, ((0, 4), (1, 8))),
        "low_u": centred(seeds[2], (LOW_MODES, NY), (LOW_MODES // 4) ** -0.5, 0.5, ((0, 32),)),
        "low_v": centred(seeds[3], (LOW_MODES, NY), (LOW_MODES // 4) ** -0.5, 0.5, ((0, 32),)),
        "low_kx": draw_low_kx(jax.random.fold_in(seeds[7], 71), 0),
        "low_kz": draw_low_kz(jax.random.fold_in(seeds[7], 71), 0),
        "tau_inverse": centred(seeds[6], (LOW_MODES, NY, NY), NY ** -0.5, 0.25, ((0, 32),)),
    }


CONTRACT_FIRST = (((0,), (0,)), ((), ()))

def axis_table(index, positions, length):
    wavenum = jnp.where(index <= KL, index, index - KL)
    phases = wavenum[:, None] * positions[None, :] % length
    angles = phases.astype(jnp.float32) * (2.0 * math.pi / length)
    return jnp.where((index <= KL)[:, None], jnp.cos(angles), jnp.sin(angles))

def mode_weight(index_x, index_z):
    return jnp.where(index_x > 0, 2.0, 1.0).astype(jnp.float32) * jnp.where(index_z > 0, 2.0, 1.0).astype(jnp.float32)

def rounded(values):
    return lax.optimization_barrier(values.astype(jnp.bfloat16)).astype(jnp.float32)

def reference(high_u, high_v, low_u, low_v, low_kx, low_kz, tau_inverse):
    unitary = 1.0 / math.sqrt(NX * NZ)
    table_z = axis_table(low_kz, jnp.arange(NZ, dtype=jnp.int32), NZ)
    stacked = jnp.concatenate([low_u, low_v], axis=1).astype(jnp.float32)
    starts = jnp.arange(NX // CX, dtype=jnp.int32) * CX

    def patterns(offset):
        table_x = axis_table(low_kx, offset + jnp.arange(CX, dtype=jnp.int32), NX)
        return rounded((table_x[:, :, None] * table_z[:, None, :]).reshape(LOW_MODES, CX * NZ))

    def first_pass(offset):
        modes_table = patterns(offset)
        coarse = lax.dot_general(modes_table, stacked, CONTRACT_FIRST, preferred_element_type=jnp.float32)
        fine_u = lax.dynamic_slice_in_dim(high_u, offset, CX, 0).reshape(CX * NZ, NY).astype(jnp.float32)
        fine_v = lax.dynamic_slice_in_dim(high_v, offset, CX, 0).reshape(CX * NZ, NY).astype(jnp.float32)
        coarse_u = coarse[:, :NY]
        coarse_v = coarse[:, NY:]
        self_term = rounded(coarse_u * coarse_v + fine_u * fine_v)
        cross_term = coarse_u * fine_v + fine_u * coarse_v
        products = jnp.concatenate([self_term, rounded(cross_term)], axis=1)
        return (jnp.dot(modes_table, products, preferred_element_type=jnp.float32), cross_term)
    partials, cross_terms = lax.map(first_pass, starts)
    projected = lax.optimization_barrier(jnp.sum(partials, axis=0)) * unitary
    forcing = projected[:, :NY].astype(jnp.bfloat16)
    cross_low = (mode_weight(low_kx, low_kz)[:, None] * projected[:, NY:]).astype(jnp.bfloat16)

    def solve(operands):
        inverse_block, forcing_block = operands
        return jnp.einsum('mij,mj->mi', inverse_block.astype(jnp.float32), forcing_block.astype(jnp.float32))
    low_response = lax.map(solve, (tau_inverse.reshape(-1, LOW_DEV, NY, NY), forcing.reshape(-1, LOW_DEV, NY)))
    low_response = low_response.reshape(LOW_MODES, NY)
    cross_wide = cross_low.astype(jnp.float32)

    def second_pass(operands):
        offset, cross_term = operands
        restored = lax.dot_general(patterns(offset), cross_wide, CONTRACT_FIRST, preferred_element_type=jnp.float32)
        return (cross_term - unitary * restored).astype(jnp.bfloat16)
    high_term = lax.map(second_pass, (starts, cross_terms)).reshape(NX, NZ, NY)
    return (high_term, low_response)
```

```python
import math

import jax
import jax.numpy as jnp
from jax import lax
from jax.experimental import pallas as pl
from jax.experimental.pallas import tpu as pltpu
from jax.sharding import PartitionSpec as P

KL = 32
LANES = 128
MESH = pl.DeviceIdType.MESH


CONTRACT_FIRST = (((0,), (0,)), ((), ()))


def axis_table(index, positions, length):
    wavenum = jnp.where(index <= KL, index, index - KL)
    phases = wavenum[:, None] * positions[None, :] % length
    angles = phases.astype(jnp.float32) * (2.0 * math.pi / length)
    return jnp.where((index <= KL)[:, None], jnp.cos(angles), jnp.sin(angles))


def mode_weight(index_x, index_z):
    return jnp.where(index_x > 0, 2.0, 1.0).astype(jnp.float32) * jnp.where(
        index_z > 0, 2.0, 1.0
    ).astype(jnp.float32)


def copy_to(src, dst, send, recv, device):
    return pltpu.make_async_remote_copy(
        src_ref=src, dst_ref=dst, send_sem=send, recv_sem=recv, device_id=device, device_id_type=MESH
    )


class Place:
    def __init__(self, groups_x, groups_z):
        self.nx, self.nc = groups_x, groups_z // 2
        self.g = lax.axis_index("gx")
        gz = lax.axis_index("gz")
        self.gz = gz
        self.c, self.k = gz // 2, gz % 2

    def partner(self):
        return (self.g, 2 * self.c + 1 - self.k)

    def along_x(self, i):
        return lax.rem(self.g + i, self.nx)

    def along_c(self, j):
        return lax.rem(self.c + j, self.nc)


def greet(p):
    barrier = pltpu.get_barrier_semaphore()
    pl.semaphore_signal(barrier, inc=1, device_id=p.partner(), device_id_type=MESH)

    @pl.loop(1, p.nx)
    def _(i):
        pl.semaphore_signal(barrier, inc=1, device_id=(p.along_x(i), p.gz), device_id_type=MESH)

    @pl.loop(1, p.nc)
    def _(j):
        pl.semaphore_signal(
            barrier, inc=1, device_id=(p.g, 2 * p.along_c(j) + p.k), device_id_type=MESH
        )

    pl.semaphore_wait(barrier, 1 + p.nx - 1 + p.nc - 1)


def gather_kernel(groups_x, groups_z, own, out, local_sem, send_x, send_c, send_p, recv):
    p = Place(groups_x, groups_z)
    greet(p)
    other = p.partner()

    def to_x(i, c, src):
        gz = 2 * c + p.k
        return copy_to(src, out.at[p.g, gz], send_x.at[i, c], recv.at[p.g, gz], (p.along_x(i), p.gz))

    def to_c(j, src):
        return copy_to(
            src, out.at[p.g, p.gz], send_c.at[j], recv.at[p.g, p.gz], (p.g, 2 * p.along_c(j) + p.k)
        )

    def to_p(g, c, src):
        gz = 2 * c + p.k
        return copy_to(src, out.at[g, gz], send_p.at[g, c], recv.at[g, gz], other)

    def arrived(g, gz):
        copy_to(own, out.at[g, gz], send_c.at[0], recv.at[g, gz], other).wait_recv()

    @pl.loop(1, p.nc)
    def _(j):
        to_c(j, own).start()

    @pl.loop(1, p.nx)
    def _(i):
        to_x(i, p.c, own).start()

    to_p(p.g, p.c, own).start()
    keep = pltpu.make_async_copy(own, out.at[p.g, p.gz], local_sem)
    keep.start()

    @pl.loop(1, p.nc)
    def _(j):
        c = p.along_c(j)
        arrived(p.g, 2 * c + p.k)

        @pl.loop(1, p.nx)
        def _(i):
            to_x(i, c, out.at[p.g, 2 * c + p.k]).start()

        to_p(p.g, c, out.at[p.g, 2 * c + p.k]).start()

    @pl.loop(0, p.nc)
    def _(j):
        c = p.along_c(j)

        @pl.loop(1, p.nx)
        def _(i):
            g = p.along_x(i)
            arrived(g, 2 * c + p.k)
            to_p(g, c, out.at[g, 2 * c + p.k]).start()

    @pl.loop(0, p.nx)
    def _(g):
        @pl.loop(0, p.nc)
        def _(c):
            arrived(g, 2 * c + 1 - p.k)

    keep.wait()

    @pl.loop(1, p.nc)
    def _(j):
        to_c(j, own).wait_send()

    @pl.loop(0, p.nc)
    def _(c):
        @pl.loop(1, p.nx)
        def _(i):
            to_x(i, c, own).wait_send()

        @pl.loop(0, p.nx)
        def _(g):
            to_p(g, c, own).wait_send()


def gather_all(block, collective_id):
    groups_x, groups_z = lax.axis_size("gx"), lax.axis_size("gz")
    rows, columns = block.shape
    chips = groups_z // 2
    dma = pltpu.SemaphoreType.DMA

    def body(*refs):
        gather_kernel(groups_x, groups_z, *refs)

    return pl.pallas_call(
        body,
        out_shape=jax.ShapeDtypeStruct((groups_x, groups_z, rows, columns), block.dtype),
        in_specs=[pl.BlockSpec(memory_space=pltpu.VMEM)],
        out_specs=pl.BlockSpec(memory_space=pltpu.VMEM),
        scratch_shapes=[
            dma,
            dma((groups_x, chips)),
            dma((chips,)),
            dma((groups_x, chips)),
            dma((groups_x, groups_z)),
        ],
        compiler_params=pltpu.CompilerParams(collective_id=collective_id, has_side_effects=True),
        name="gather",
    )(block).reshape(groups_x * groups_z * rows, columns)


def scatter_kernel(
    groups_x, groups_z, part, out, pair, sums, from_x, acc, sent_c, from_c,
    send_p, recv_p, send_x, recv_x, send_c, recv_c,
):
    p = Place(groups_x, groups_z)
    greet(p)
    other = p.partner()

    def to_p(g):
        return copy_to(part.at[g, :, 1 - p.k], pair.at[g], send_p.at[g], recv_p.at[g], other)

    def to_x(i):
        g = p.along_x(i)
        return copy_to(sums.at[g], from_x.at[p.g], send_x.at[g], recv_x.at[p.g], (g, p.gz))

    def to_c(j):
        c = p.along_c(j)
        return copy_to(sent_c.at[c], from_c.at[p.c], send_c.at[c], recv_c.at[p.c], (p.g, 2 * c + p.k))

    @pl.loop(1, p.nx + 1)
    def _(i):
        to_p(p.along_x(i)).start()

    def chip_sum(g):
        to_p(g).wait_recv()
        return part[g, :, p.k].astype(jnp.float32) + pair[g].astype(jnp.float32)

    @pl.loop(1, p.nx)
    def _(i):
        g = p.along_x(i)
        sums[g] = chip_sum(g).astype(sums.dtype)
        to_x(i).start()

    acc[...] = chip_sum(p.g)

    @pl.loop(1, p.nx)
    def _(i):
        g = p.along_x(i)
        copy_to(sums.at[g], from_x.at[g], send_x.at[g], recv_x.at[g], other).wait_recv()
        acc[...] += from_x[g].astype(jnp.float32)

    @pl.loop(1, p.nc)
    def _(j):
        c = p.along_c(j)
        sent_c[c] = acc[c].astype(sent_c.dtype)
        to_c(j).start()

    out[...] = acc[p.c]

    @pl.loop(1, p.nc)
    def _(j):
        c = p.along_c(j)
        copy_to(sent_c.at[c], from_c.at[c], send_c.at[c], recv_c.at[c], other).wait_recv()
        out[...] += from_c[c].astype(jnp.float32)

    @pl.loop(0, p.nx)
    def _(g):
        to_p(g).wait_send()

    @pl.loop(1, p.nx)
    def _(i):
        to_x(i).wait_send()

    @pl.loop(1, p.nc)
    def _(j):
        to_c(j).wait_send()


def scatter_sum(part, collective_id):
    groups_x, groups_z = lax.axis_size("gx"), lax.axis_size("gz")
    modes, columns = part.shape
    rows = modes // (groups_x * groups_z)
    chips = groups_z // 2
    dma = pltpu.SemaphoreType.DMA
    kind = part.dtype

    def body(*refs):
        scatter_kernel(groups_x, groups_z, *refs)

    return pl.pallas_call(
        body,
        out_shape=jax.ShapeDtypeStruct((rows, columns), jnp.float32),
        in_specs=[pl.BlockSpec(memory_space=pltpu.VMEM)],
        out_specs=pl.BlockSpec(memory_space=pltpu.VMEM),
        scratch_shapes=[
            pltpu.VMEM((groups_x, chips, rows, columns), kind),
            pltpu.VMEM((groups_x, chips, rows, columns), kind),
            pltpu.VMEM((groups_x, chips, rows, columns), kind),
            pltpu.VMEM((chips, rows, columns), jnp.float32),
            pltpu.VMEM((chips, rows, columns), kind),
            pltpu.VMEM((chips, rows, columns), kind),
            dma((groups_x,)),
            dma((groups_x,)),
            dma((groups_x,)),
            dma((groups_x,)),
            dma((chips,)),
            dma((chips,)),
        ],
        compiler_params=pltpu.CompilerParams(collective_id=collective_id, has_side_effects=True),
        name="scatter",
    )(part.reshape(groups_x, chips, 2, rows, columns))


def on_device(high_u, high_v, low_u, low_v, low_kx, low_kz, tau_inverse):
    cells_x, cells_z, levels = high_u.shape
    groups_x = lax.axis_size("gx")
    groups_z = lax.axis_size("gz")
    length_x = groups_x * cells_x
    length_z = groups_z * cells_z
    points = cells_x * cells_z
    unitary = 1.0 / math.sqrt(length_x * length_z)
    where_x = lax.axis_index("gx") * cells_x + jnp.arange(cells_x, dtype=jnp.int32)
    where_z = lax.axis_index("gz") * cells_z + jnp.arange(cells_z, dtype=jnp.int32)

    lane = jnp.arange(LANES, dtype=jnp.int32)[None, :]
    labels = jnp.where(lane == 0, low_kx[:, None], low_kz[:, None]).astype(jnp.bfloat16)
    block = jnp.concatenate([low_u, low_v, labels], axis=1)
    every = gather_all(block, 0)
    index_x = every[:, 2 * levels].astype(jnp.int32)
    index_z = every[:, 2 * levels + 1].astype(jnp.int32)
    table_x = axis_table(index_x, where_x, length_x)
    table_z = axis_table(index_z, where_z, length_z)
    patterns = (
        (table_x[:, :, None] * table_z[:, None, :])
        .reshape(index_x.shape[0], points)
        .astype(jnp.bfloat16)
    )
    coarse = lax.dot_general(
        patterns, every[:, : 2 * levels], CONTRACT_FIRST, preferred_element_type=jnp.float32
    )
    fine_u = high_u.reshape(points, levels)
    fine_v = high_v.reshape(points, levels)
    coarse_u = coarse[:, :levels]
    coarse_v = coarse[:, levels:]
    self_term = (coarse_u * coarse_v + fine_u.astype(jnp.float32) * fine_v).astype(jnp.bfloat16)
    cross_term = coarse_u * fine_v + fine_u * coarse_v
    cross_round = cross_term.astype(jnp.bfloat16)
    products = jnp.concatenate([self_term, cross_round], axis=1)
    part = jnp.dot(patterns, products, preferred_element_type=jnp.float32) * unitary
    totals = scatter_sum(part.astype(jnp.bfloat16), 1)
    own_weight = mode_weight(low_kx, low_kz)[:, None]
    forcing = totals[:, :levels]
    cross_low = (own_weight * totals[:, levels:]).astype(jnp.bfloat16)
    restored = lax.dot_general(
        patterns, gather_all(cross_low, 2), CONTRACT_FIRST, preferred_element_type=jnp.float32
    )
    high_term = (
        (cross_term - unitary * restored).astype(jnp.bfloat16).reshape(cells_x, cells_z, levels)
    )
    low_response = jnp.einsum(
        "mij,mj->mi", tau_inverse, forcing.astype(jnp.bfloat16), preferred_element_type=jnp.float32
    )
    return (high_term, low_response)


def solution(mesh):
    placed = (
        P("gx", "gz", None),
        P("gx", "gz", None),
        P(("gx", "gz"), None),
        P(("gx", "gz"), None),
        P(("gx", "gz")),
        P(("gx", "gz")),
        P(("gx", "gz"), None, None),
    )
    return jax.shard_map(
        on_device,
        mesh=mesh,
        in_specs=placed,
        out_specs=(P("gx", "gz", None), P(("gx", "gz"), None)),
        check_vma=False,
    )
```

```python
import math

import jax
import jax.numpy as jnp
from jax import lax
from jax.experimental import pallas as pl
from jax.experimental.pallas import tpu as pltpu
from jax.sharding import PartitionSpec as P

KL = 32
LANES = 128
MESH = pl.DeviceIdType.MESH


NT = (((1,), (1,)), ((), ()))


def mode_weight(index_x, index_z):
    return jnp.where(index_x > 0, 2.0, 1.0).astype(jnp.float32) * jnp.where(
        index_z > 0, 2.0, 1.0
    ).astype(jnp.float32)


def wrapped(phase, length):
    return phase & (length - 1) if length & (length - 1) == 0 else lax.rem(phase, length)


def copy_to(src, dst, send, recv, device):
    return pltpu.make_async_remote_copy(
        src_ref=src, dst_ref=dst, send_sem=send, recv_sem=recv, device_id=device, device_id_type=MESH
    )


class Place:
    def __init__(self, groups_x, groups_z):
        self.nx, self.nc = groups_x, groups_z // 2
        self.g = lax.axis_index("gx")
        gz = lax.axis_index("gz")
        self.gz = gz
        self.c, self.k = gz // 2, gz % 2

    def partner(self):
        return (self.g, 2 * self.c + 1 - self.k)

    def along_x(self, i):
        return lax.rem(self.g + i, self.nx)

    def along_c(self, j):
        return lax.rem(self.c + j, self.nc)


def greet(p):
    barrier = pltpu.get_barrier_semaphore()
    pl.semaphore_signal(barrier, inc=1, device_id=p.partner(), device_id_type=MESH)

    @pl.loop(1, p.nx)
    def _(i):
        pl.semaphore_signal(barrier, inc=1, device_id=(p.along_x(i), p.gz), device_id_type=MESH)

    @pl.loop(1, p.nc)
    def _(j):
        pl.semaphore_signal(
            barrier, inc=1, device_id=(p.g, 2 * p.along_c(j) + p.k), device_id_type=MESH
        )

    pl.semaphore_wait(barrier, 1 + p.nx - 1 + p.nc - 1)


class Gather:
    def __init__(self, p, out, send_x, send_c, send_p, recv):
        self.p, self.out = p, out
        self.send_x, self.send_c, self.send_p, self.recv = send_x, send_c, send_p, recv

    def at(self, g, gz):
        return self.out.at[g, gz]

    def to_x(self, i, c):
        p, gz = self.p, 2 * c + self.p.k
        return copy_to(
            self.at(p.g, gz), self.at(p.g, gz), self.send_x.at[i, c], self.recv.at[p.g, gz],
            (p.along_x(i), p.gz),
        )

    def to_c(self, j):
        p = self.p
        return copy_to(
            self.at(p.g, p.gz), self.at(p.g, p.gz), self.send_c.at[j], self.recv.at[p.g, p.gz],
            (p.g, 2 * p.along_c(j) + p.k),
        )

    def to_p(self, g, c):
        gz = 2 * c + self.p.k
        return copy_to(
            self.at(g, gz), self.at(g, gz), self.send_p.at[g, c], self.recv.at[g, gz],
            self.p.partner(),
        )

    def arrived(self, g, gz):
        copy_to(
            self.at(g, gz), self.at(g, gz), self.send_c.at[0], self.recv.at[g, gz],
            self.p.partner(),
        ).wait_recv()

    def start(self):
        p = self.p

        @pl.loop(1, p.nc)
        def _(j):
            self.to_c(j).start()

        @pl.loop(1, p.nx)
        def _(i):
            self.to_x(i, p.c).start()

        self.to_p(p.g, p.c).start()

    def relay_c(self):
        p = self.p

        @pl.loop(1, p.nc)
        def _(j):
            c = p.along_c(j)
            self.arrived(p.g, 2 * c + p.k)

            @pl.loop(1, p.nx)
            def _(i):
                self.to_x(i, c).start()

            self.to_p(p.g, c).start()

    def relay_x(self):
        p = self.p

        @pl.loop(0, p.nc)
        def _(j):
            c = p.along_c(j)

            @pl.loop(1, p.nx)
            def _(i):
                g = p.along_x(i)
                self.arrived(g, 2 * c + p.k)
                self.to_p(g, c).start()

    def from_partner(self, g):
        p = self.p

        @pl.loop(0, p.nc)
        def _(j):
            self.arrived(g, 2 * p.along_c(j) + 1 - p.k)

    def drain(self):
        p = self.p

        @pl.loop(1, p.nc)
        def _(j):
            self.to_c(j).wait_send()

        @pl.loop(0, p.nc)
        def _(c):
            @pl.loop(1, p.nx)
            def _(i):
                self.to_x(i, c).wait_send()

            @pl.loop(0, p.nx)
            def _(g):
                self.to_p(g, c).wait_send()


class Scatter:
    def __init__(self, p, part, pair, sums, from_x, acc, sent_c, from_c, sems):
        self.p, self.part, self.pair, self.sums, self.from_x = p, part, pair, sums, from_x
        self.acc, self.sent_c, self.from_c = acc, sent_c, from_c
        self.send_p, self.recv_p, self.send_x, self.recv_x, self.send_c, self.recv_c = sems

    def to_p(self, g):
        return copy_to(
            self.part.at[g, :, 1 - self.p.k], self.pair.at[g], self.send_p.at[g],
            self.recv_p.at[g], self.p.partner(),
        )

    def to_x(self, i):
        p = self.p
        g = p.along_x(i)
        return copy_to(
            self.sums.at[g], self.from_x.at[p.g], self.send_x.at[g], self.recv_x.at[p.g], (g, p.gz)
        )

    def to_c(self, j):
        p = self.p
        c = p.along_c(j)
        return copy_to(
            self.sent_c.at[c], self.from_c.at[p.c], self.send_c.at[c], self.recv_c.at[p.c],
            (p.g, 2 * c + p.k),
        )

    def chip_sum(self, g):
        self.to_p(g).wait_recv()
        return self.part[g, :, self.p.k] + self.pair[g]

    def across_x(self):
        p = self.p

        @pl.loop(1, p.nx)
        def _(i):
            g = p.along_x(i)
            self.sums[g] = self.chip_sum(g).astype(self.sums.dtype)
            self.to_x(i).start()

        self.acc[...] = self.chip_sum(p.g)

    def across_c(self):
        p = self.p

        @pl.loop(1, p.nx)
        def _(i):
            g = p.along_x(i)
            copy_to(
                self.sums.at[g], self.from_x.at[g], self.send_x.at[g], self.recv_x.at[g], p.partner()
            ).wait_recv()
            self.acc[...] += self.from_x[g].astype(jnp.float32)

        @pl.loop(1, p.nc)
        def _(j):
            c = p.along_c(j)
            self.sent_c[c] = self.acc[c].astype(self.sent_c.dtype)
            self.to_c(j).start()

    def total(self):
        p = self.p

        @pl.loop(1, p.nc)
        def _(j):
            c = p.along_c(j)
            copy_to(
                self.sent_c.at[c], self.from_c.at[c], self.send_c.at[c], self.recv_c.at[c],
                p.partner(),
            ).wait_recv()
            self.acc[p.c] += self.from_c[c].astype(jnp.float32)

        return self.acc[p.c]

    def drain(self):
        p = self.p

        @pl.loop(0, p.nx)
        def _(g):
            self.to_p(g).wait_send()

        @pl.loop(1, p.nx)
        def _(i):
            self.to_x(i).wait_send()

        @pl.loop(1, p.nc)
        def _(j):
            self.to_c(j).wait_send()


SCATTER_SEMS = 6


def step_kernel(
    groups_x, groups_z,
    high_u, high_v, low_u, low_v, labels, weight, tau,
    high_term, response,
    fine_u, fine_v, inverse, every, tables_t, tables, cross, products, mirror, answer, all_cross,
    load, first_sems, second_sems, cross_buffers, self_buffers,
):
    p = Place(groups_x, groups_z)
    cells_x, cells_z, levels = fine_u.shape
    points = cells_x * cells_z
    rows = low_u.shape[0]
    group = groups_z * rows
    lengths = (groups_x * cells_x, groups_z * cells_z)
    unitary = 1.0 / math.sqrt(lengths[0] * lengths[1])

    mine = every.at[p.g, p.gz]
    own = [
        pltpu.make_async_copy(low_u, mine.at[:, pl.ds(0, levels)], load.at[0]),
        pltpu.make_async_copy(low_v, mine.at[:, pl.ds(levels, levels)], load.at[1]),
        pltpu.make_async_copy(labels, mine.at[:, pl.ds(2 * levels, LANES)], load.at[2]),
    ]
    fields = [
        pltpu.make_async_copy(high_u, fine_u, load.at[3]),
        pltpu.make_async_copy(high_v, fine_v, load.at[4]),
        pltpu.make_async_copy(tau, inverse, load.at[5]),
    ]
    for copy in own + fields:
        copy.start()
    greet(p)
    for copy in own:
        copy.wait()
    first = Gather(p, every, *first_sems)
    first.start()

    lane = lax.broadcasted_iota(jnp.int32, (group, LANES), 1)
    on_x = lane < cells_x
    place = jnp.where(on_x, p.g * cells_x + lane, p.gz * cells_z + lane - cells_x)
    first.relay_c()
    first.relay_x()

    def build(i, _):
        g = p.along_x(i)
        first.from_partner(g)
        index = every[g, :, :, pl.ds(2 * levels, LANES)].reshape(group, LANES)
        index = index.astype(jnp.float32).astype(jnp.int32)
        even = index <= KL
        phase = jnp.where(even, index, index - KL) * place

        def angle(length):
            shifted = jnp.where(even, phase, phase + (length - length // 4))
            return wrapped(shifted, length).astype(jnp.float32) * (2.0 * math.pi / length)

        table = jnp.cos(jnp.where(on_x, angle(lengths[0]), angle(lengths[1])))
        turned = table.T
        along_z = turned[cells_x : cells_x + cells_z, :]
        at = pl.ds(pl.multiple_of(g * group, LANES), group)
        for x in range(cells_x):
            slab = turned[x : x + 1, :] * along_z
            tables_t[pl.ds(x * cells_z, cells_z), at] = slab.astype(tables_t.dtype)
        return 0

    lax.fori_loop(0, p.nx, build, 0)

    def turn(g, _):
        at = pl.ds(pl.multiple_of(g * group, LANES), group)
        tables[at, :] = tables_t[:, at].T
        return 0

    lax.fori_loop(0, p.nx, turn, 0)

    fields[0].wait()
    fields[1].wait()
    modes = groups_x * group
    block = 256 if points % 256 == 0 else points
    planes = block // cells_z

    def multiply(b, _):
        at = pl.ds(pl.multiple_of(b * block, block), block)
        held = every[:, :, :, pl.ds(0, 2 * levels)].reshape(modes, 2 * levels)
        coarse = jnp.dot(tables_t[at, :], held, preferred_element_type=jnp.float32)
        coarse_u, coarse_v = coarse[:, :levels], coarse[:, levels:]
        u = fine_u[pl.ds(b * planes, planes)].reshape(block, levels).astype(jnp.float32)
        v = fine_v[pl.ds(b * planes, planes)].reshape(block, levels).astype(jnp.float32)
        mixed = coarse_u * v + u * coarse_v
        cross[at, :] = mixed
        products[0, at, :] = mixed.astype(products.dtype)
        products[1, at, :] = (coarse_u * coarse_v + u * v).astype(products.dtype)
        return 0

    lax.fori_loop(0, points // block, multiply, 0)

    def project(scatter, which):
        def one(i, _):
            g = p.along_x(i)
            at = pl.ds(pl.multiple_of(g * group, LANES), group)
            scatter.part[g] = jnp.dot(
                tables[at, :], products[which], preferred_element_type=jnp.float32
            ).reshape(p.nc, 2, rows, levels)
            scatter.to_p(g).start()
            return 0

        lax.fori_loop(1, p.nx + 1, one, 0)

    crossed = Scatter(p, *cross_buffers)
    selfed = Scatter(p, *self_buffers)
    project(crossed, 0)
    crossed.across_x()
    project(selfed, 1)
    selfed.across_x()
    crossed.across_c()
    selfed.across_c()
    all_cross[p.g, p.gz] = (weight[:, 0:1] * (crossed.total() * unitary)).astype(all_cross.dtype)
    second = Gather(p, all_cross, *second_sems)
    second.start()
    forcing = (selfed.total() * unitary).astype(jnp.bfloat16)
    fields[2].wait()
    row = lax.broadcasted_iota(jnp.int32, (rows, levels), 0)
    answer[...] = jnp.zeros_like(answer)

    def solve(m, _):
        full = lax.dot_general(forcing, inverse[m], NT, preferred_element_type=jnp.float32)
        answer[...] += jnp.where(row == m, full, 0.0)
        return 0

    lax.fori_loop(0, rows // 2, solve, 0)
    second.relay_c()
    lax.fori_loop(rows // 2, rows, solve, 0)
    second.relay_x()
    response[...] = answer[...]

    @pl.loop(0, p.nx)
    def _(g):
        second.from_partner(g)

    def finish(b, _):
        at = pl.ds(pl.multiple_of(b * block, block), block)
        held = all_cross[...].reshape(modes, levels)
        restored = jnp.dot(tables_t[at, :], held, preferred_element_type=jnp.float32)
        part = (cross[at, :] - unitary * restored).astype(mirror.dtype)
        mirror[pl.ds(b * planes, planes)] = part.reshape(planes, cells_z, levels)
        writing(b).start()
        return 0

    def writing(b):
        at = pl.ds(b * planes, planes)
        return pltpu.make_async_copy(mirror.at[at], high_term.at[at], load.at[6 + b])

    lax.fori_loop(0, points // block, finish, 0)
    first.drain()
    second.drain()
    crossed.drain()
    selfed.drain()

    @pl.loop(0, points // block)
    def _(b):
        writing(b).wait()


def on_device(high_u, high_v, low_u, low_v, low_kx, low_kz, tau_inverse):
    cells_x, cells_z, levels = high_u.shape
    groups_x, groups_z = lax.axis_size("gx"), lax.axis_size("gz")
    chips, rows = groups_z // 2, low_u.shape[0]
    points = cells_x * cells_z
    modes = groups_x * groups_z * rows
    lane = jnp.arange(LANES, dtype=jnp.int32)[None, :]
    labels = jnp.where(lane < cells_x, low_kx[:, None], low_kz[:, None]).astype(jnp.bfloat16)
    weight = jnp.broadcast_to(mode_weight(low_kx, low_kz)[:, None], (rows, LANES))
    dma = pltpu.SemaphoreType.DMA
    narrow, wide = jnp.bfloat16, jnp.float32
    gather_sems = [
        dma((groups_x, chips)), dma((chips,)), dma((groups_x, chips)), dma((groups_x, groups_z)),
    ]
    scatter_buffers = [
        pltpu.VMEM((groups_x, chips, 2, rows, levels), wide),
        pltpu.VMEM((groups_x, chips, rows, levels), wide),
        pltpu.VMEM((groups_x, chips, rows, levels), narrow),
        pltpu.VMEM((groups_x, chips, rows, levels), narrow),
        pltpu.VMEM((chips, rows, levels), wide),
        pltpu.VMEM((chips, rows, levels), narrow),
        pltpu.VMEM((chips, rows, levels), narrow),
        [dma((groups_x,))] * 4 + [dma((chips,))] * 2,
    ]
    vmem, anywhere = pl.BlockSpec(memory_space=pltpu.VMEM), pl.BlockSpec(memory_space=pl.ANY)

    def body(*refs):
        step_kernel(groups_x, groups_z, *refs)

    return pl.pallas_call(
        body,
        out_shape=(
            jax.ShapeDtypeStruct(high_u.shape, narrow),
            jax.ShapeDtypeStruct((rows, levels), wide),
        ),
        in_specs=[anywhere, anywhere, vmem, vmem, vmem, vmem, anywhere],
        out_specs=(anywhere, vmem),
        scratch_shapes=[
            pltpu.VMEM(high_u.shape, narrow),
            pltpu.VMEM(high_u.shape, narrow),
            pltpu.VMEM(tau_inverse.shape, narrow),
            pltpu.VMEM((groups_x, groups_z, rows, 2 * levels + LANES), narrow),
            pltpu.VMEM((points, modes), narrow),
            pltpu.VMEM((modes, points), narrow),
            pltpu.VMEM((points, levels), wide),
            pltpu.VMEM((2, points, levels), narrow),
            pltpu.VMEM(high_u.shape, narrow),
            pltpu.VMEM((rows, levels), wide),
            pltpu.VMEM((groups_x, groups_z, rows, levels), narrow),
            dma((7 + points // 256,)),
            gather_sems,
            gather_sems,
            scatter_buffers,
            scatter_buffers,
        ],
        compiler_params=pltpu.CompilerParams(
            collective_id=0, has_side_effects=True, vmem_limit_bytes=60 * 1024 * 1024
        ),
        name="step",
    )(high_u, high_v, low_u, low_v, labels, weight, tau_inverse)


def solution(mesh):
    placed = (
        P("gx", "gz", None),
        P("gx", "gz", None),
        P(("gx", "gz"), None),
        P(("gx", "gz"), None),
        P(("gx", "gz")),
        P(("gx", "gz")),
        P(("gx", "gz"), None, None),
    )
    return jax.shard_map(
        on_device,
        mesh=mesh,
        in_specs=placed,
        out_specs=(P("gx", "gz", None), P(("gx", "gz"), None)),
        check_vma=False,
    )
```

```python
import math

import jax
import jax.numpy as jnp
from jax import lax
from jax.experimental import pallas as pl
from jax.experimental.pallas import tpu as pltpu
from jax.sharding import PartitionSpec as P

KL = 32
LANES = 128
MESH = pl.DeviceIdType.MESH


NT = (((1,), (1,)), ((), ()))


def wrapped(phase, length):
    return phase & (length - 1) if length & (length - 1) == 0 else lax.rem(phase, length)


def row_block(points):
    return 256 if points % 256 == 0 else points


def copy_to(src, dst, send, recv, device):
    return pltpu.make_async_remote_copy(
        src_ref=src, dst_ref=dst, send_sem=send, recv_sem=recv, device_id=device, device_id_type=MESH
    )


class Place:
    def __init__(self, groups_x, groups_z):
        self.nx, self.nc = groups_x, groups_z // 2
        self.g = lax.axis_index("gx")
        gz = lax.axis_index("gz")
        self.gz = gz
        self.c, self.k = gz // 2, gz % 2

    def partner(self):
        return (self.g, 2 * self.c + 1 - self.k)

    def along_x(self, i):
        return lax.rem(self.g + i, self.nx)

    def along_c(self, j):
        return lax.rem(self.c + j, self.nc)


def greet(p):
    barrier = pltpu.get_barrier_semaphore()
    pl.semaphore_signal(barrier, inc=1, device_id=p.partner(), device_id_type=MESH)

    @pl.loop(1, p.nx)
    def _(i):
        pl.semaphore_signal(barrier, inc=1, device_id=(p.along_x(i), p.gz), device_id_type=MESH)

    @pl.loop(1, p.nc)
    def _(j):
        pl.semaphore_signal(
            barrier, inc=1, device_id=(p.g, 2 * p.along_c(j) + p.k), device_id_type=MESH
        )

    pl.semaphore_wait(barrier, 1 + p.nx - 1 + p.nc - 1)


class Gather:
    def __init__(self, p, out, send_x, send_c, send_p, recv):
        self.p, self.out = p, out
        self.send_x, self.send_c, self.send_p, self.recv = send_x, send_c, send_p, recv

    def at(self, g, gz):
        return self.out.at[g, gz]

    def to_x(self, i, c):
        p, gz = self.p, 2 * c + self.p.k
        return copy_to(
            self.at(p.g, gz), self.at(p.g, gz), self.send_x.at[i, c], self.recv.at[p.g, gz],
            (p.along_x(i), p.gz),
        )

    def to_c(self, j):
        p = self.p
        return copy_to(
            self.at(p.g, p.gz), self.at(p.g, p.gz), self.send_c.at[j], self.recv.at[p.g, p.gz],
            (p.g, 2 * p.along_c(j) + p.k),
        )

    def to_p(self, g, c):
        gz = 2 * c + self.p.k
        return copy_to(
            self.at(g, gz), self.at(g, gz), self.send_p.at[g, c], self.recv.at[g, gz],
            self.p.partner(),
        )

    def arrived(self, g, gz):
        copy_to(
            self.at(g, gz), self.at(g, gz), self.send_c.at[0], self.recv.at[g, gz],
            self.p.partner(),
        ).wait_recv()

    def start(self):
        p = self.p

        @pl.loop(1, p.nc)
        def _(j):
            self.to_c(j).start()

        @pl.loop(1, p.nx)
        def _(i):
            self.to_x(i, p.c).start()

        self.to_p(p.g, p.c).start()

    def relay_c(self):
        p = self.p

        @pl.loop(1, p.nc)
        def _(j):
            c = p.along_c(j)
            self.arrived(p.g, 2 * c + p.k)

            @pl.loop(1, p.nx)
            def _(i):
                self.to_x(i, c).start()

            self.to_p(p.g, c).start()

    def relay_x(self):
        p = self.p

        @pl.loop(0, p.nc)
        def _(j):
            c = p.along_c(j)

            @pl.loop(1, p.nx)
            def _(i):
                g = p.along_x(i)
                self.arrived(g, 2 * c + p.k)
                self.to_p(g, c).start()

    def from_partner(self, g):
        p = self.p

        @pl.loop(0, p.nc)
        def _(j):
            self.arrived(g, 2 * p.along_c(j) + 1 - p.k)

    def drain(self):
        p = self.p

        @pl.loop(1, p.nc)
        def _(j):
            self.to_c(j).wait_send()

        @pl.loop(0, p.nc)
        def _(c):
            @pl.loop(1, p.nx)
            def _(i):
                self.to_x(i, c).wait_send()

            @pl.loop(0, p.nx)
            def _(g):
                self.to_p(g, c).wait_send()


class Scatter:
    def __init__(self, p, part, pair, sums, from_x, acc, sent_c, from_c, sems):
        self.p, self.part, self.pair, self.sums, self.from_x = p, part, pair, sums, from_x
        self.acc, self.sent_c, self.from_c = acc, sent_c, from_c
        self.send_p, self.recv_p, self.send_x, self.recv_x, self.send_c, self.recv_c = sems

    def to_p(self, g):
        return copy_to(
            self.part.at[g, :, 1 - self.p.k], self.pair.at[g], self.send_p.at[g],
            self.recv_p.at[g], self.p.partner(),
        )

    def to_x(self, i):
        p = self.p
        g = p.along_x(i)
        return copy_to(
            self.sums.at[g], self.from_x.at[p.g], self.send_x.at[g], self.recv_x.at[p.g], (g, p.gz)
        )

    def to_c(self, j):
        p = self.p
        c = p.along_c(j)
        return copy_to(
            self.sent_c.at[c], self.from_c.at[p.c], self.send_c.at[c], self.recv_c.at[p.c],
            (p.g, 2 * c + p.k),
        )

    def chip_sum(self, g):
        self.to_p(g).wait_recv()
        return self.part[g, :, self.p.k] + self.pair[g]

    def across_x(self):
        p = self.p

        @pl.loop(1, p.nx)
        def _(i):
            g = p.along_x(i)
            self.sums[g] = self.chip_sum(g).astype(self.sums.dtype)
            self.to_x(i).start()

        self.acc[...] = self.chip_sum(p.g)

    def across_c(self):
        p = self.p

        @pl.loop(1, p.nx)
        def _(i):
            g = p.along_x(i)
            copy_to(
                self.sums.at[g], self.from_x.at[g], self.send_x.at[g], self.recv_x.at[g], p.partner()
            ).wait_recv()
            self.acc[...] += self.from_x[g].astype(jnp.float32)

        @pl.loop(1, p.nc)
        def _(j):
            c = p.along_c(j)
            self.sent_c[c] = self.acc[c].astype(self.sent_c.dtype)
            self.to_c(j).start()

    def total(self):
        p = self.p

        @pl.loop(1, p.nc)
        def _(j):
            c = p.along_c(j)
            copy_to(
                self.sent_c.at[c], self.from_c.at[c], self.send_c.at[c], self.recv_c.at[c],
                p.partner(),
            ).wait_recv()
            self.acc[p.c] += self.from_c[c].astype(jnp.float32)

        return self.acc[p.c]

    def drain(self):
        p = self.p

        @pl.loop(0, p.nx)
        def _(g):
            self.to_p(g).wait_send()

        @pl.loop(1, p.nx)
        def _(i):
            self.to_x(i).wait_send()

        @pl.loop(1, p.nc)
        def _(j):
            self.to_c(j).wait_send()


LIMIT_ONE = 48 * 1024 * 1024
LIMIT_TWO = 16 * 1024 * 1024


def step_kernel(
    groups_x, groups_z,
    high_u, high_v, low_u, low_v, low_kx, low_kz, tau,
    cross, tables_t, all_cross, answer,
    fine_u, fine_v, inverse, every, tables, products,
    load, first_sems, second_sems, cross_buffers, self_buffers,
):
    p = Place(groups_x, groups_z)
    cells_x, cells_z, levels = fine_u.shape
    points = cells_x * cells_z
    rows = low_u.shape[0]
    group = groups_z * rows
    lengths = (groups_x * cells_x, groups_z * cells_z)
    unitary = 1.0 / math.sqrt(lengths[0] * lengths[1])

    mine = every.at[p.g, p.gz]
    own = [
        pltpu.make_async_copy(low_u, mine.at[:, pl.ds(0, levels)], load.at[0]),
        pltpu.make_async_copy(low_v, mine.at[:, pl.ds(levels, levels)], load.at[1]),
    ]
    fields = [
        pltpu.make_async_copy(high_u, fine_u, load.at[3]),
        pltpu.make_async_copy(high_v, fine_v, load.at[4]),
        pltpu.make_async_copy(tau, inverse, load.at[5]),
    ]
    for copy in own + fields:
        copy.start()
    slot = lax.broadcasted_iota(jnp.int32, (rows, rows), 0)
    straight = slot == lax.broadcasted_iota(jnp.int32, (rows, rows), 1)

    def upright(line):
        spread = jnp.broadcast_to(line[...].astype(jnp.float32), (rows, rows))
        return jnp.sum(jnp.where(straight, spread, 0.0), axis=1, keepdims=True)

    kx, kz = upright(low_kx), upright(low_kz)
    weight = jnp.where(kx > 0, 2.0, 1.0) * jnp.where(kz > 0, 2.0, 1.0)
    first_lanes = lax.broadcasted_iota(jnp.int32, (rows, LANES), 1) < cells_x
    every[p.g, p.gz, :, pl.ds(2 * levels, LANES)] = jnp.where(first_lanes, kx, kz).astype(every.dtype)
    greet(p)
    for copy in own:
        copy.wait()
    first = Gather(p, every, *first_sems)
    first.start()

    lane = lax.broadcasted_iota(jnp.int32, (group, LANES), 1)
    on_x = lane < cells_x
    place = jnp.where(on_x, p.g * cells_x + lane, p.gz * cells_z + lane - cells_x)
    first.relay_c()
    first.relay_x()

    def build(i, _):
        g = p.along_x(i)
        first.from_partner(g)
        index = every[g, :, :, pl.ds(2 * levels, LANES)].reshape(group, LANES)
        index = index.astype(jnp.float32).astype(jnp.int32)
        even = index <= KL
        phase = jnp.where(even, index, index - KL) * place

        def angle(length):
            shifted = jnp.where(even, phase, phase + (length - length // 4))
            return wrapped(shifted, length).astype(jnp.float32) * (2.0 * math.pi / length)

        table = jnp.cos(jnp.where(on_x, angle(lengths[0]), angle(lengths[1])))
        turned = table.T
        along_z = turned[cells_x : cells_x + cells_z, :]
        at = pl.ds(pl.multiple_of(g * group, LANES), group)
        for x in range(cells_x):
            slab = turned[x : x + 1, :] * along_z
            tables_t[pl.ds(x * cells_z, cells_z), at] = slab.astype(tables_t.dtype)
        return 0

    lax.fori_loop(0, p.nx, build, 0)

    def turn(g, _):
        at = pl.ds(pl.multiple_of(g * group, LANES), group)
        tables[at, :] = tables_t[:, at].T
        return 0

    lax.fori_loop(0, p.nx, turn, 0)

    fields[0].wait()
    fields[1].wait()
    modes = groups_x * group
    block = row_block(points)
    planes = block // cells_z

    def multiply(b, _):
        at = pl.ds(pl.multiple_of(b * block, block), block)
        held = every[:, :, :, pl.ds(0, 2 * levels)].reshape(modes, 2 * levels)
        coarse = jnp.dot(tables_t[at, :], held, preferred_element_type=jnp.float32)
        coarse_u, coarse_v = coarse[:, :levels], coarse[:, levels:]
        u = fine_u[pl.ds(b * planes, planes)].reshape(block, levels).astype(jnp.float32)
        v = fine_v[pl.ds(b * planes, planes)].reshape(block, levels).astype(jnp.float32)
        mixed = coarse_u * v + u * coarse_v
        cross[at, :] = mixed
        products[0, at, :] = mixed.astype(products.dtype)
        products[1, at, :] = (coarse_u * coarse_v + u * v).astype(products.dtype)
        return 0

    lax.fori_loop(0, points // block, multiply, 0)

    def project(scatter, which):
        def one(i, _):
            g = p.along_x(i)
            at = pl.ds(pl.multiple_of(g * group, LANES), group)
            scatter.part[g] = jnp.dot(
                tables[at, :], products[which], preferred_element_type=jnp.float32
            ).reshape(p.nc, 2, rows, levels)
            scatter.to_p(g).start()
            return 0

        lax.fori_loop(1, p.nx + 1, one, 0)

    crossed = Scatter(p, *cross_buffers)
    selfed = Scatter(p, *self_buffers)
    project(crossed, 0)
    crossed.across_x()
    project(selfed, 1)
    selfed.across_x()
    crossed.across_c()
    selfed.across_c()
    all_cross[p.g, p.gz] = (weight * (crossed.total() * unitary)).astype(all_cross.dtype)
    second = Gather(p, all_cross, *second_sems)
    second.start()
    forcing = (selfed.total() * unitary).astype(jnp.bfloat16)
    fields[2].wait()
    row = lax.broadcasted_iota(jnp.int32, (rows, levels), 0)
    answer[...] = jnp.zeros_like(answer)

    def solve(m, _):
        full = lax.dot_general(forcing, inverse[m], NT, preferred_element_type=jnp.float32)
        answer[...] += jnp.where(row == m, full, 0.0)
        return 0

    lax.fori_loop(0, rows // 2, solve, 0)
    second.relay_c()
    lax.fori_loop(rows // 2, rows, solve, 0)
    second.relay_x()

    @pl.loop(0, p.nx)
    def _(g):
        second.from_partner(g)

    first.drain()
    second.drain()
    crossed.drain()
    selfed.drain()


def finish_kernel(unitary, cross, tables_t, all_cross, answer, high_term, response, mirror, sems):
    points, levels = cross.shape
    cells_z = high_term.shape[1]
    block = row_block(points)
    planes = block // cells_z
    modes = tables_t.shape[1]
    response[...] = answer[...]

    def writing(b):
        at = pl.ds(b * planes, planes)
        return pltpu.make_async_copy(mirror.at[at], high_term.at[at], sems.at[b])

    def finish(b, _):
        at = pl.ds(pl.multiple_of(b * block, block), block)
        held = all_cross[...].reshape(modes, levels)
        restored = jnp.dot(tables_t[at, :], held, preferred_element_type=jnp.float32)
        part = (cross[at, :] - unitary * restored).astype(mirror.dtype)
        mirror[pl.ds(b * planes, planes)] = part.reshape(planes, cells_z, levels)
        writing(b).start()
        return 0

    lax.fori_loop(0, points // block, finish, 0)

    @pl.loop(0, points // block)
    def _(b):
        writing(b).wait()


def on_device(high_u, high_v, low_u, low_v, low_kx, low_kz, tau_inverse):
    cells_x, cells_z, levels = high_u.shape
    groups_x, groups_z = lax.axis_size("gx"), lax.axis_size("gz")
    chips, rows = groups_z // 2, low_u.shape[0]
    points = cells_x * cells_z
    modes = groups_x * groups_z * rows
    dma = pltpu.SemaphoreType.DMA
    narrow, wide = jnp.bfloat16, jnp.float32
    gather_sems = [
        dma((groups_x, chips)), dma((chips,)), dma((groups_x, chips)), dma((groups_x, groups_z)),
    ]
    scatter_buffers = [
        pltpu.VMEM((groups_x, chips, 2, rows, levels), wide),
        pltpu.VMEM((groups_x, chips, rows, levels), wide),
        pltpu.VMEM((groups_x, chips, rows, levels), narrow),
        pltpu.VMEM((groups_x, chips, rows, levels), narrow),
        pltpu.VMEM((chips, rows, levels), wide),
        pltpu.VMEM((chips, rows, levels), narrow),
        pltpu.VMEM((chips, rows, levels), narrow),
        [dma((groups_x,))] * 4 + [dma((chips,))] * 2,
    ]
    vmem, hbm = pl.BlockSpec(memory_space=pltpu.VMEM), pl.BlockSpec(memory_space=pltpu.HBM)

    def body(*refs):
        step_kernel(groups_x, groups_z, *refs)

    cross, tables_t, all_cross, answer = pl.pallas_call(
        body,
        out_shape=(
            jax.ShapeDtypeStruct((points, levels), wide),
            jax.ShapeDtypeStruct((points, modes), narrow),
            jax.ShapeDtypeStruct((groups_x, groups_z, rows, levels), narrow),
            jax.ShapeDtypeStruct((rows, levels), wide),
        ),
        in_specs=[hbm, hbm, hbm, hbm, vmem, vmem, hbm],
        out_specs=(vmem, vmem, vmem, vmem),
        scratch_shapes=[
            pltpu.VMEM(high_u.shape, narrow),
            pltpu.VMEM(high_u.shape, narrow),
            pltpu.VMEM(tau_inverse.shape, narrow),
            pltpu.VMEM((groups_x, groups_z, rows, 2 * levels + LANES), narrow),
            pltpu.VMEM((modes, points), narrow),
            pltpu.VMEM((2, points, levels), narrow),
            dma((6,)),
            gather_sems,
            gather_sems,
            scatter_buffers,
            scatter_buffers,
        ],
        compiler_params=pltpu.CompilerParams(
            collective_id=0, has_side_effects=True, vmem_limit_bytes=LIMIT_ONE
        ),
        name="step",
    )(high_u, high_v, low_u, low_v, low_kx.reshape(1, rows), low_kz.reshape(1, rows), tau_inverse)
    unitary = 1.0 / math.sqrt(groups_x * cells_x * groups_z * cells_z)

    def last(*refs):
        finish_kernel(unitary, *refs)

    return pl.pallas_call(
        last,
        out_shape=(
            jax.ShapeDtypeStruct(high_u.shape, narrow),
            jax.ShapeDtypeStruct((rows, levels), wide),
        ),
        in_specs=[vmem, vmem, vmem, vmem],
        out_specs=(hbm, vmem),
        scratch_shapes=[pltpu.VMEM(high_u.shape, narrow), dma((points // row_block(points),))],
        compiler_params=pltpu.CompilerParams(vmem_limit_bytes=LIMIT_TWO),
        name="finish",
    )(cross, tables_t, all_cross, answer)


def solution(mesh):
    placed = (
        P("gx", "gz", None),
        P("gx", "gz", None),
        P(("gx", "gz"), None),
        P(("gx", "gz"), None),
        P(("gx", "gz")),
        P(("gx", "gz")),
        P(("gx", "gz"), None, None),
    )
    return jax.shard_map(
        on_device,
        mesh=mesh,
        in_specs=placed,
        out_specs=(P("gx", "gz", None), P(("gx", "gz"), None)),
        check_vma=False,
    )
```

```python
import math

import jax
import jax.numpy as jnp
from jax import lax
from jax.experimental import pallas as pl
from jax.experimental.pallas import tpu as pltpu
from jax.sharding import PartitionSpec as P

KL = 32
LANES = 128
MESH = pl.DeviceIdType.MESH


NT = (((1,), (1,)), ((), ()))


def wrapped(phase, length):
    return phase & (length - 1) if length & (length - 1) == 0 else lax.rem(phase, length)


def row_block(points):
    return 256 if points % 256 == 0 else points


def copy_to(src, dst, send, recv, device):
    return pltpu.make_async_remote_copy(
        src_ref=src, dst_ref=dst, send_sem=send, recv_sem=recv, device_id=device, device_id_type=MESH
    )


class Place:
    def __init__(self, groups_x, groups_z):
        self.nx, self.nc = groups_x, groups_z // 2
        self.g = lax.axis_index("gx")
        gz = lax.axis_index("gz")
        self.gz = gz
        self.c, self.k = gz // 2, gz % 2

    def partner(self):
        return (self.g, 2 * self.c + 1 - self.k)

    def along_x(self, i):
        return lax.rem(self.g + i, self.nx)

    def along_c(self, j):
        return lax.rem(self.c + j, self.nc)


def greet(p):
    barrier = pltpu.get_barrier_semaphore()
    pl.semaphore_signal(barrier, inc=1, device_id=p.partner(), device_id_type=MESH)

    @pl.loop(1, p.nx)
    def _(i):
        pl.semaphore_signal(barrier, inc=1, device_id=(p.along_x(i), p.gz), device_id_type=MESH)

    @pl.loop(1, p.nc)
    def _(j):
        pl.semaphore_signal(
            barrier, inc=1, device_id=(p.g, 2 * p.along_c(j) + p.k), device_id_type=MESH
        )

    pl.semaphore_wait(barrier, 1 + p.nx - 1 + p.nc - 1)


class Gather:
    def __init__(self, p, out, send_x, send_c, send_p, recv):
        self.p, self.out = p, out
        self.send_x, self.send_c, self.send_p, self.recv = send_x, send_c, send_p, recv

    def at(self, g, gz):
        return self.out.at[g, gz]

    def to_x(self, i, c):
        p, gz = self.p, 2 * c + self.p.k
        return copy_to(
            self.at(p.g, gz), self.at(p.g, gz), self.send_x.at[i, c], self.recv.at[p.g, gz],
            (p.along_x(i), p.gz),
        )

    def to_c(self, j):
        p = self.p
        return copy_to(
            self.at(p.g, p.gz), self.at(p.g, p.gz), self.send_c.at[j], self.recv.at[p.g, p.gz],
            (p.g, 2 * p.along_c(j) + p.k),
        )

    def to_p(self, g, c):
        gz = 2 * c + self.p.k
        return copy_to(
            self.at(g, gz), self.at(g, gz), self.send_p.at[g, c], self.recv.at[g, gz],
            self.p.partner(),
        )

    def arrived(self, g, gz):
        copy_to(
            self.at(g, gz), self.at(g, gz), self.send_c.at[0], self.recv.at[g, gz],
            self.p.partner(),
        ).wait_recv()

    def start(self):
        p = self.p

        @pl.loop(1, p.nc)
        def _(j):
            self.to_c(j).start()

        @pl.loop(1, p.nx)
        def _(i):
            self.to_x(i, p.c).start()

        self.to_p(p.g, p.c).start()

    def relay_c(self):
        p = self.p

        @pl.loop(1, p.nc)
        def _(j):
            c = p.along_c(j)
            self.arrived(p.g, 2 * c + p.k)

            @pl.loop(1, p.nx)
            def _(i):
                self.to_x(i, c).start()

            self.to_p(p.g, c).start()

    def relay_x(self):
        p = self.p

        @pl.loop(0, p.nc)
        def _(j):
            c = p.along_c(j)

            @pl.loop(1, p.nx)
            def _(i):
                g = p.along_x(i)
                self.arrived(g, 2 * c + p.k)
                self.to_p(g, c).start()

    def from_partner(self, g):
        p = self.p

        @pl.loop(0, p.nc)
        def _(j):
            self.arrived(g, 2 * p.along_c(j) + 1 - p.k)

    def drain(self):
        p = self.p

        @pl.loop(1, p.nc)
        def _(j):
            self.to_c(j).wait_send()

        @pl.loop(0, p.nc)
        def _(c):
            @pl.loop(1, p.nx)
            def _(i):
                self.to_x(i, c).wait_send()

            @pl.loop(0, p.nx)
            def _(g):
                self.to_p(g, c).wait_send()


class Scatter:
    def __init__(self, p, part, pair, sums, from_x, acc, sent_c, from_c, sems):
        self.p, self.part, self.pair, self.sums, self.from_x = p, part, pair, sums, from_x
        self.acc, self.sent_c, self.from_c = acc, sent_c, from_c
        self.send_p, self.recv_p, self.send_x, self.recv_x, self.send_c, self.recv_c = sems

    def to_p(self, g):
        return copy_to(
            self.part.at[g, :, 1 - self.p.k], self.pair.at[g], self.send_p.at[g],
            self.recv_p.at[g], self.p.partner(),
        )

    def to_x(self, i):
        p = self.p
        g = p.along_x(i)
        return copy_to(
            self.sums.at[g], self.from_x.at[p.g], self.send_x.at[g], self.recv_x.at[p.g], (g, p.gz)
        )

    def to_c(self, j):
        p = self.p
        c = p.along_c(j)
        return copy_to(
            self.sent_c.at[c], self.from_c.at[p.c], self.send_c.at[c], self.recv_c.at[p.c],
            (p.g, 2 * c + p.k),
        )

    def chip_sum(self, g):
        self.to_p(g).wait_recv()
        return self.part[g, :, self.p.k] + self.pair[g]

    def across_x(self):
        p = self.p

        @pl.loop(1, p.nx)
        def _(i):
            g = p.along_x(i)
            self.sums[g] = self.chip_sum(g).astype(self.sums.dtype)
            self.to_x(i).start()

        self.acc[...] = self.chip_sum(p.g)

    def across_c(self):
        p = self.p

        @pl.loop(1, p.nx)
        def _(i):
            g = p.along_x(i)
            copy_to(
                self.sums.at[g], self.from_x.at[g], self.send_x.at[g], self.recv_x.at[g], p.partner()
            ).wait_recv()
            self.acc[...] += self.from_x[g].astype(jnp.float32)

        @pl.loop(1, p.nc)
        def _(j):
            c = p.along_c(j)
            self.sent_c[c] = self.acc[c].astype(self.sent_c.dtype)
            self.to_c(j).start()

    def total(self):
        p = self.p

        @pl.loop(1, p.nc)
        def _(j):
            c = p.along_c(j)
            copy_to(
                self.sent_c.at[c], self.from_c.at[c], self.send_c.at[c], self.recv_c.at[c],
                p.partner(),
            ).wait_recv()
            self.acc[p.c] += self.from_c[c].astype(jnp.float32)

        return self.acc[p.c]

    def drain(self):
        p = self.p

        @pl.loop(0, p.nx)
        def _(g):
            self.to_p(g).wait_send()

        @pl.loop(1, p.nx)
        def _(i):
            self.to_x(i).wait_send()

        @pl.loop(1, p.nc)
        def _(j):
            self.to_c(j).wait_send()


LIMIT_ONE = 48 * 1024 * 1024
LIMIT_TWO = 16 * 1024 * 1024


def step_kernel(
    groups_x, groups_z,
    high_u, high_v, low_u, low_v, low_kx, low_kz, tau,
    cross, tables_t, all_cross, answer,
    fine_u, fine_v, inverse, every, tables, products, lines,
    load, first_sems, second_sems, cross_buffers, self_buffers,
):
    p = Place(groups_x, groups_z)
    cells_x, cells_z, levels = fine_u.shape
    points = cells_x * cells_z
    rows = low_u.shape[0]
    group = groups_z * rows
    lengths = (groups_x * cells_x, groups_z * cells_z)
    unitary = 1.0 / math.sqrt(lengths[0] * lengths[1])

    mine = every.at[p.g, p.gz]
    own = [
        pltpu.make_async_copy(low_u, mine.at[:, pl.ds(0, levels)], load.at[0]),
        pltpu.make_async_copy(low_v, mine.at[:, pl.ds(levels, levels)], load.at[1]),
    ]
    fields = [
        pltpu.make_async_copy(high_u, fine_u, load.at[3]),
        pltpu.make_async_copy(high_v, fine_v, load.at[4]),
        pltpu.make_async_copy(tau, inverse, load.at[5]),
    ]
    indices = [
        pltpu.make_async_copy(low_kx, lines.at[0], load.at[2]),
        pltpu.make_async_copy(low_kz, lines.at[1], load.at[6]),
    ]
    for copy in indices + own + fields:
        copy.start()
    slot = lax.broadcasted_iota(jnp.int32, (rows, rows), 0)
    straight = slot == lax.broadcasted_iota(jnp.int32, (rows, rows), 1)

    def upright(line):
        spread = jnp.broadcast_to(line.astype(jnp.float32), (rows, rows))
        return jnp.sum(jnp.where(straight, spread, 0.0), axis=1, keepdims=True)

    for copy in indices:
        copy.wait()
    kx, kz = upright(lines[0]), upright(lines[1])
    weight = jnp.where(kx > 0, 2.0, 1.0) * jnp.where(kz > 0, 2.0, 1.0)
    first_lanes = lax.broadcasted_iota(jnp.int32, (rows, LANES), 1) < cells_x
    every[p.g, p.gz, :, pl.ds(2 * levels, LANES)] = jnp.where(first_lanes, kx, kz).astype(every.dtype)
    greet(p)
    for copy in own:
        copy.wait()
    first = Gather(p, every, *first_sems)
    first.start()

    lane = lax.broadcasted_iota(jnp.int32, (group, LANES), 1)
    on_x = lane < cells_x
    place = jnp.where(on_x, p.g * cells_x + lane, p.gz * cells_z + lane - cells_x)
    first.relay_c()
    first.relay_x()

    def build(i, _):
        g = p.along_x(i)
        first.from_partner(g)
        index = every[g, :, :, pl.ds(2 * levels, LANES)].reshape(group, LANES)
        index = index.astype(jnp.float32).astype(jnp.int32)
        even = index <= KL
        phase = jnp.where(even, index, index - KL) * place

        def angle(length):
            shifted = jnp.where(even, phase, phase + (length - length // 4))
            return wrapped(shifted, length).astype(jnp.float32) * (2.0 * math.pi / length)

        table = jnp.cos(jnp.where(on_x, angle(lengths[0]), angle(lengths[1])))
        turned = table.T
        along_z = turned[cells_x : cells_x + cells_z, :]
        at = pl.ds(pl.multiple_of(g * group, LANES), group)
        for x in range(cells_x):
            slab = turned[x : x + 1, :] * along_z
            tables_t[pl.ds(x * cells_z, cells_z), at] = slab.astype(tables_t.dtype)
        return 0

    lax.fori_loop(0, p.nx, build, 0)

    def turn(g, _):
        at = pl.ds(pl.multiple_of(g * group, LANES), group)
        tables[at, :] = tables_t[:, at].T
        return 0

    lax.fori_loop(0, p.nx, turn, 0)

    fields[0].wait()
    fields[1].wait()
    modes = groups_x * group
    block = row_block(points)
    planes = block // cells_z

    def multiply(b, _):
        at = pl.ds(pl.multiple_of(b * block, block), block)
        held = every[:, :, :, pl.ds(0, 2 * levels)].reshape(modes, 2 * levels)
        coarse = jnp.dot(tables_t[at, :], held, preferred_element_type=jnp.float32)
        coarse_u, coarse_v = coarse[:, :levels], coarse[:, levels:]
        u = fine_u[pl.ds(b * planes, planes)].reshape(block, levels).astype(jnp.float32)
        v = fine_v[pl.ds(b * planes, planes)].reshape(block, levels).astype(jnp.float32)
        mixed = coarse_u * v + u * coarse_v
        cross[at, :] = mixed
        products[0, at, :] = mixed.astype(products.dtype)
        products[1, at, :] = (coarse_u * coarse_v + u * v).astype(products.dtype)
        return 0

    lax.fori_loop(0, points // block, multiply, 0)

    def project(scatter, which):
        def one(i, _):
            g = p.along_x(i)
            at = pl.ds(pl.multiple_of(g * group, LANES), group)
            scatter.part[g] = jnp.dot(
                tables[at, :], products[which], preferred_element_type=jnp.float32
            ).reshape(p.nc, 2, rows, levels)
            scatter.to_p(g).start()
            return 0

        lax.fori_loop(1, p.nx + 1, one, 0)

    crossed = Scatter(p, *cross_buffers)
    selfed = Scatter(p, *self_buffers)
    project(crossed, 0)
    crossed.across_x()
    project(selfed, 1)
    selfed.across_x()
    crossed.across_c()
    selfed.across_c()
    all_cross[p.g, p.gz] = (weight * (crossed.total() * unitary)).astype(all_cross.dtype)
    second = Gather(p, all_cross, *second_sems)
    second.start()
    forcing = (selfed.total() * unitary).astype(jnp.bfloat16)
    fields[2].wait()
    row = lax.broadcasted_iota(jnp.int32, (rows, levels), 0)
    answer[...] = jnp.zeros_like(answer)

    def solve(m, _):
        full = lax.dot_general(forcing, inverse[m], NT, preferred_element_type=jnp.float32)
        answer[...] += jnp.where(row == m, full, 0.0)
        return 0

    lax.fori_loop(0, rows // 2, solve, 0)
    second.relay_c()
    lax.fori_loop(rows // 2, rows, solve, 0)
    second.relay_x()

    @pl.loop(0, p.nx)
    def _(g):
        second.from_partner(g)

    first.drain()
    second.drain()
    crossed.drain()
    selfed.drain()


def finish_kernel(unitary, cross, tables_t, all_cross, answer, high_term, response, mirror, sems):
    points, levels = cross.shape
    cells_z = high_term.shape[1]
    block = row_block(points)
    planes = block // cells_z
    modes = tables_t.shape[1]
    response[...] = answer[...]

    def writing(b):
        at = pl.ds(b * planes, planes)
        return pltpu.make_async_copy(mirror.at[at], high_term.at[at], sems.at[b])

    def finish(b, _):
        at = pl.ds(pl.multiple_of(b * block, block), block)
        held = all_cross[...].reshape(modes, levels)
        restored = jnp.dot(tables_t[at, :], held, preferred_element_type=jnp.float32)
        part = (cross[at, :] - unitary * restored).astype(mirror.dtype)
        mirror[pl.ds(b * planes, planes)] = part.reshape(planes, cells_z, levels)
        writing(b).start()
        return 0

    lax.fori_loop(0, points // block, finish, 0)

    @pl.loop(0, points // block)
    def _(b):
        writing(b).wait()


def on_device(high_u, high_v, low_u, low_v, low_kx, low_kz, tau_inverse):
    cells_x, cells_z, levels = high_u.shape
    groups_x, groups_z = lax.axis_size("gx"), lax.axis_size("gz")
    chips, rows = groups_z // 2, low_u.shape[0]
    points = cells_x * cells_z
    modes = groups_x * groups_z * rows
    dma = pltpu.SemaphoreType.DMA
    narrow, wide = jnp.bfloat16, jnp.float32
    gather_sems = [
        dma((groups_x, chips)), dma((chips,)), dma((groups_x, chips)), dma((groups_x, groups_z)),
    ]
    scatter_buffers = [
        pltpu.VMEM((groups_x, chips, 2, rows, levels), wide),
        pltpu.VMEM((groups_x, chips, rows, levels), wide),
        pltpu.VMEM((groups_x, chips, rows, levels), narrow),
        pltpu.VMEM((groups_x, chips, rows, levels), narrow),
        pltpu.VMEM((chips, rows, levels), wide),
        pltpu.VMEM((chips, rows, levels), narrow),
        pltpu.VMEM((chips, rows, levels), narrow),
        [dma((groups_x,))] * 4 + [dma((chips,))] * 2,
    ]
    vmem, hbm = pl.BlockSpec(memory_space=pltpu.VMEM), pl.BlockSpec(memory_space=pltpu.HBM)

    def body(*refs):
        step_kernel(groups_x, groups_z, *refs)

    cross, tables_t, all_cross, answer = pl.pallas_call(
        body,
        out_shape=(
            jax.ShapeDtypeStruct((points, levels), wide),
            jax.ShapeDtypeStruct((points, modes), narrow),
            jax.ShapeDtypeStruct((groups_x, groups_z, rows, levels), narrow),
            jax.ShapeDtypeStruct((rows, levels), wide),
        ),
        in_specs=[hbm] * 7,
        out_specs=(vmem, vmem, vmem, vmem),
        scratch_shapes=[
            pltpu.VMEM(high_u.shape, narrow),
            pltpu.VMEM(high_u.shape, narrow),
            pltpu.VMEM(tau_inverse.shape, narrow),
            pltpu.VMEM((groups_x, groups_z, rows, 2 * levels + LANES), narrow),
            pltpu.VMEM((modes, points), narrow),
            pltpu.VMEM((2, points, levels), narrow),
            pltpu.VMEM((2, 1, rows), jnp.int32),
            dma((7,)),
            gather_sems,
            gather_sems,
            scatter_buffers,
            scatter_buffers,
        ],
        compiler_params=pltpu.CompilerParams(
            collective_id=0, has_side_effects=True, vmem_limit_bytes=LIMIT_ONE
        ),
        name="step",
    )(
        *(
            pltpu.with_memory_space_constraint(array, pltpu.HBM)
            for array in (
                high_u, high_v, low_u, low_v, low_kx.reshape(1, rows), low_kz.reshape(1, rows),
                tau_inverse,
            )
        )
    )
    unitary = 1.0 / math.sqrt(groups_x * cells_x * groups_z * cells_z)

    def last(*refs):
        finish_kernel(unitary, *refs)

    return pl.pallas_call(
        last,
        out_shape=(
            jax.ShapeDtypeStruct(high_u.shape, narrow),
            jax.ShapeDtypeStruct((rows, levels), wide),
        ),
        in_specs=[vmem, vmem, vmem, vmem],
        out_specs=(hbm, vmem),
        scratch_shapes=[pltpu.VMEM(high_u.shape, narrow), dma((points // row_block(points),))],
        compiler_params=pltpu.CompilerParams(vmem_limit_bytes=LIMIT_TWO),
        name="finish",
    )(cross, tables_t, all_cross, answer)


def solution(mesh):
    placed = (
        P("gx", "gz", None),
        P("gx", "gz", None),
        P(("gx", "gz"), None),
        P(("gx", "gz"), None),
        P(("gx", "gz")),
        P(("gx", "gz")),
        P(("gx", "gz"), None, None),
    )
    return jax.shard_map(
        on_device,
        mesh=mesh,
        in_specs=placed,
        out_specs=(P("gx", "gz", None), P(("gx", "gz"), None)),
        check_vma=False,
    )
```

```python
import math

import jax
import jax.numpy as jnp
from jax import lax
from jax.experimental import pallas as pl
from jax.experimental.pallas import tpu as pltpu
from jax.sharding import PartitionSpec as P

KL = 32
LANES = 128
MESH = pl.DeviceIdType.MESH


NT = (((1,), (1,)), ((), ()))


def wrapped(phase, length):
    return phase & (length - 1) if length & (length - 1) == 0 else lax.rem(phase, length)


def row_block(points):
    return 256 if points % 256 == 0 else points


def copy_to(src, dst, send, recv, device):
    return pltpu.make_async_remote_copy(
        src_ref=src, dst_ref=dst, send_sem=send, recv_sem=recv, device_id=device, device_id_type=MESH
    )


class Place:
    def __init__(self, groups_x, groups_z):
        self.nx, self.nc = groups_x, groups_z // 2
        self.g = lax.axis_index("gx")
        gz = lax.axis_index("gz")
        self.gz = gz
        self.c, self.k = gz // 2, gz % 2

    def partner(self):
        return (self.g, 2 * self.c + 1 - self.k)

    def along_x(self, i):
        return lax.rem(self.g + i, self.nx)

    def along_c(self, j):
        return lax.rem(self.c + j, self.nc)


def greet(p):
    barrier = pltpu.get_barrier_semaphore()
    pl.semaphore_signal(barrier, inc=1, device_id=p.partner(), device_id_type=MESH)

    @pl.loop(1, p.nx)
    def _(i):
        pl.semaphore_signal(barrier, inc=1, device_id=(p.along_x(i), p.gz), device_id_type=MESH)

    @pl.loop(1, p.nc)
    def _(j):
        pl.semaphore_signal(
            barrier, inc=1, device_id=(p.g, 2 * p.along_c(j) + p.k), device_id_type=MESH
        )

    return lambda: pl.semaphore_wait(barrier, 1 + p.nx - 1 + p.nc - 1)


class Gather:
    def __init__(self, p, out, send_x, send_c, send_p, recv):
        self.p, self.out = p, out
        self.send_x, self.send_c, self.send_p, self.recv = send_x, send_c, send_p, recv

    def at(self, g, gz):
        return self.out.at[g, gz]

    def to_x(self, i, c):
        p, gz = self.p, 2 * c + self.p.k
        return copy_to(
            self.at(p.g, gz), self.at(p.g, gz), self.send_x.at[i, c], self.recv.at[p.g, gz],
            (p.along_x(i), p.gz),
        )

    def to_c(self, j):
        p = self.p
        return copy_to(
            self.at(p.g, p.gz), self.at(p.g, p.gz), self.send_c.at[j], self.recv.at[p.g, p.gz],
            (p.g, 2 * p.along_c(j) + p.k),
        )

    def to_p(self, g, c):
        gz = 2 * c + self.p.k
        return copy_to(
            self.at(g, gz), self.at(g, gz), self.send_p.at[g, c], self.recv.at[g, gz],
            self.p.partner(),
        )

    def arrived(self, g, gz):
        copy_to(
            self.at(g, gz), self.at(g, gz), self.send_c.at[0], self.recv.at[g, gz],
            self.p.partner(),
        ).wait_recv()

    def start(self):
        p = self.p

        @pl.loop(1, p.nc)
        def _(j):
            self.to_c(j).start()

        @pl.loop(1, p.nx)
        def _(i):
            self.to_x(i, p.c).start()

        self.to_p(p.g, p.c).start()

    def relay_c(self):
        p = self.p

        @pl.loop(1, p.nc)
        def _(j):
            c = p.along_c(j)
            self.arrived(p.g, 2 * c + p.k)

            @pl.loop(1, p.nx)
            def _(i):
                self.to_x(i, c).start()

            self.to_p(p.g, c).start()

    def relay_x(self):
        p = self.p

        @pl.loop(0, p.nc)
        def _(j):
            c = p.along_c(j)

            @pl.loop(1, p.nx)
            def _(i):
                g = p.along_x(i)
                self.arrived(g, 2 * c + p.k)
                self.to_p(g, c).start()

    def from_partner(self, g):
        p = self.p

        @pl.loop(0, p.nc)
        def _(j):
            self.arrived(g, 2 * p.along_c(j) + 1 - p.k)

    def drain(self):
        p = self.p

        @pl.loop(1, p.nc)
        def _(j):
            self.to_c(j).wait_send()

        @pl.loop(0, p.nc)
        def _(c):
            @pl.loop(1, p.nx)
            def _(i):
                self.to_x(i, c).wait_send()

            @pl.loop(0, p.nx)
            def _(g):
                self.to_p(g, c).wait_send()


class Scatter:
    def __init__(self, p, part, pair, sums, from_x, acc, sent_c, from_c, sems):
        self.p, self.part, self.pair, self.sums, self.from_x = p, part, pair, sums, from_x
        self.acc, self.sent_c, self.from_c = acc, sent_c, from_c
        self.send_p, self.recv_p, self.send_x, self.recv_x, self.send_c, self.recv_c = sems

    def to_p(self, g):
        return copy_to(
            self.part.at[g, :, 1 - self.p.k], self.pair.at[g], self.send_p.at[g],
            self.recv_p.at[g], self.p.partner(),
        )

    def to_x(self, i):
        p = self.p
        g = p.along_x(i)
        return copy_to(
            self.sums.at[g], self.from_x.at[p.g], self.send_x.at[g], self.recv_x.at[p.g], (g, p.gz)
        )

    def to_c(self, j):
        p = self.p
        c = p.along_c(j)
        return copy_to(
            self.sent_c.at[c], self.from_c.at[p.c], self.send_c.at[c], self.recv_c.at[p.c],
            (p.g, 2 * c + p.k),
        )

    def chip_sum(self, g):
        self.to_p(g).wait_recv()
        return self.part[g, :, self.p.k] + self.pair[g]

    def across_x(self):
        p = self.p

        @pl.loop(1, p.nx)
        def _(i):
            g = p.along_x(i)
            self.sums[g] = self.chip_sum(g).astype(self.sums.dtype)
            self.to_x(i).start()

        self.acc[...] = self.chip_sum(p.g)

    def across_c(self):
        p = self.p

        @pl.loop(1, p.nx)
        def _(i):
            g = p.along_x(i)
            copy_to(
                self.sums.at[g], self.from_x.at[g], self.send_x.at[g], self.recv_x.at[g], p.partner()
            ).wait_recv()
            self.acc[...] += self.from_x[g].astype(jnp.float32)

        @pl.loop(1, p.nc)
        def _(j):
            c = p.along_c(j)
            self.sent_c[c] = self.acc[c].astype(self.sent_c.dtype)
            self.to_c(j).start()

    def total(self):
        p = self.p

        @pl.loop(1, p.nc)
        def _(j):
            c = p.along_c(j)
            copy_to(
                self.sent_c.at[c], self.from_c.at[c], self.send_c.at[c], self.recv_c.at[c],
                p.partner(),
            ).wait_recv()
            self.acc[p.c] += self.from_c[c].astype(jnp.float32)

        return self.acc[p.c]

    def drain(self):
        p = self.p

        @pl.loop(0, p.nx)
        def _(g):
            self.to_p(g).wait_send()

        @pl.loop(1, p.nx)
        def _(i):
            self.to_x(i).wait_send()

        @pl.loop(1, p.nc)
        def _(j):
            self.to_c(j).wait_send()


LIMIT_ONE = 48 * 1024 * 1024
LIMIT_TWO = 16 * 1024 * 1024


def step_kernel(
    groups_x, groups_z,
    high_u, high_v, low_u, low_v, low_kx, low_kz, tau,
    cross, tables_t, all_cross, answer,
    fine_u, fine_v, inverse, every, tables, products, lines, marks,
    load, ahead_sems, first_sems, second_sems, cross_buffers, self_buffers,
):
    p = Place(groups_x, groups_z)
    all_here = greet(p)
    cells_x, cells_z, levels = fine_u.shape
    points = cells_x * cells_z
    rows = low_u.shape[0]
    group = groups_z * rows
    lengths = (groups_x * cells_x, groups_z * cells_z)
    unitary = 1.0 / math.sqrt(lengths[0] * lengths[1])

    mine = every.at[p.g, p.gz]
    own = [
        pltpu.make_async_copy(low_u, mine.at[:, pl.ds(0, levels)], load.at[0]),
        pltpu.make_async_copy(low_v, mine.at[:, pl.ds(levels, levels)], load.at[1]),
    ]
    fields = [
        pltpu.make_async_copy(high_u, fine_u, load.at[3]),
        pltpu.make_async_copy(high_v, fine_v, load.at[4]),
        pltpu.make_async_copy(tau, inverse, load.at[5]),
    ]
    indices = [
        pltpu.make_async_copy(low_kx, lines.at[0], load.at[2]),
        pltpu.make_async_copy(low_kz, lines.at[1], load.at[6]),
    ]
    for copy in indices + own + fields:
        copy.start()
    slot = lax.broadcasted_iota(jnp.int32, (rows, rows), 0)
    straight = slot == lax.broadcasted_iota(jnp.int32, (rows, rows), 1)

    def upright(line):
        spread = jnp.broadcast_to(line.astype(jnp.float32), (rows, rows))
        return jnp.sum(jnp.where(straight, spread, 0.0), axis=1, keepdims=True)

    for copy in indices:
        copy.wait()
    kx, kz = upright(lines[0]), upright(lines[1])
    weight = jnp.where(kx > 0, 2.0, 1.0) * jnp.where(kz > 0, 2.0, 1.0)
    first_lanes = lax.broadcasted_iota(jnp.int32, (rows, LANES), 1) < cells_x
    marks[p.g, p.gz] = jnp.where(first_lanes, kx, kz).astype(marks.dtype)
    all_here()
    ahead = Gather(p, marks, *ahead_sems)
    ahead.start()
    for copy in own:
        copy.wait()
    first = Gather(p, every, *first_sems)
    first.start()

    lane = lax.broadcasted_iota(jnp.int32, (group, LANES), 1)
    on_x = lane < cells_x
    place = jnp.where(on_x, p.g * cells_x + lane, p.gz * cells_z + lane - cells_x)
    ahead.relay_c()
    first.relay_c()
    ahead.relay_x()

    def build(i, _):
        g = p.along_x(i)
        ahead.from_partner(g)
        index = marks[g].reshape(group, LANES)
        index = index.astype(jnp.float32).astype(jnp.int32)
        even = index <= KL
        phase = jnp.where(even, index, index - KL) * place

        def angle(length):
            shifted = jnp.where(even, phase, phase + (length - length // 4))
            return wrapped(shifted, length).astype(jnp.float32) * (2.0 * math.pi / length)

        table = jnp.cos(jnp.where(on_x, angle(lengths[0]), angle(lengths[1])))
        turned = table.T
        along_z = turned[cells_x : cells_x + cells_z, :]
        at = pl.ds(pl.multiple_of(g * group, LANES), group)
        for x in range(cells_x):
            slab = turned[x : x + 1, :] * along_z
            tables_t[pl.ds(x * cells_z, cells_z), at] = slab.astype(tables_t.dtype)
        return 0

    lax.fori_loop(0, p.nx, build, 0)

    def turn(g, _):
        at = pl.ds(pl.multiple_of(g * group, LANES), group)
        tables[at, :] = tables_t[:, at].T
        return 0

    lax.fori_loop(0, p.nx, turn, 0)
    first.relay_x()

    @pl.loop(0, p.nx)
    def _(g):
        first.from_partner(g)

    fields[0].wait()
    fields[1].wait()
    modes = groups_x * group
    block = row_block(points)
    planes = block // cells_z

    def multiply(b, _):
        at = pl.ds(pl.multiple_of(b * block, block), block)
        held = every[...].reshape(modes, 2 * levels)
        coarse = jnp.dot(tables_t[at, :], held, preferred_element_type=jnp.float32)
        coarse_u, coarse_v = coarse[:, :levels], coarse[:, levels:]
        u = fine_u[pl.ds(b * planes, planes)].reshape(block, levels).astype(jnp.float32)
        v = fine_v[pl.ds(b * planes, planes)].reshape(block, levels).astype(jnp.float32)
        mixed = coarse_u * v + u * coarse_v
        cross[at, :] = mixed
        products[0, at, :] = mixed.astype(products.dtype)
        products[1, at, :] = (coarse_u * coarse_v + u * v).astype(products.dtype)
        return 0

    lax.fori_loop(0, points // block, multiply, 0)

    def project(scatter, which):
        def one(i, _):
            g = p.along_x(i)
            at = pl.ds(pl.multiple_of(g * group, LANES), group)
            scatter.part[g] = jnp.dot(
                tables[at, :], products[which], preferred_element_type=jnp.float32
            ).reshape(p.nc, 2, rows, levels)
            scatter.to_p(g).start()
            return 0

        lax.fori_loop(1, p.nx + 1, one, 0)

    crossed = Scatter(p, *cross_buffers)
    selfed = Scatter(p, *self_buffers)
    project(crossed, 0)
    crossed.across_x()
    project(selfed, 1)
    selfed.across_x()
    crossed.across_c()
    selfed.across_c()
    all_cross[p.g, p.gz] = (weight * (crossed.total() * unitary)).astype(all_cross.dtype)
    second = Gather(p, all_cross, *second_sems)
    second.start()
    forcing = (selfed.total() * unitary).astype(jnp.bfloat16)
    fields[2].wait()
    row = lax.broadcasted_iota(jnp.int32, (rows, levels), 0)
    answer[...] = jnp.zeros_like(answer)

    def solve(m, _):
        full = lax.dot_general(forcing, inverse[m], NT, preferred_element_type=jnp.float32)
        answer[...] += jnp.where(row == m, full, 0.0)
        return 0

    lax.fori_loop(0, rows // 2, solve, 0)
    second.relay_c()
    lax.fori_loop(rows // 2, rows, solve, 0)
    second.relay_x()

    @pl.loop(0, p.nx)
    def _(g):
        second.from_partner(g)

    ahead.drain()
    first.drain()
    second.drain()
    crossed.drain()
    selfed.drain()


def finish_kernel(unitary, cross, tables_t, all_cross, answer, high_term, response, mirror, sems):
    points, levels = cross.shape
    cells_z = high_term.shape[1]
    block = row_block(points)
    planes = block // cells_z
    modes = tables_t.shape[1]
    response[...] = answer[...]

    def writing(b):
        at = pl.ds(b * planes, planes)
        return pltpu.make_async_copy(mirror.at[at], high_term.at[at], sems.at[b])

    def finish(b, _):
        at = pl.ds(pl.multiple_of(b * block, block), block)
        held = all_cross[...].reshape(modes, levels)
        restored = jnp.dot(tables_t[at, :], held, preferred_element_type=jnp.float32)
        part = (cross[at, :] - unitary * restored).astype(mirror.dtype)
        mirror[pl.ds(b * planes, planes)] = part.reshape(planes, cells_z, levels)
        writing(b).start()
        return 0

    lax.fori_loop(0, points // block, finish, 0)

    @pl.loop(0, points // block)
    def _(b):
        writing(b).wait()


def on_device(high_u, high_v, low_u, low_v, low_kx, low_kz, tau_inverse):
    cells_x, cells_z, levels = high_u.shape
    groups_x, groups_z = lax.axis_size("gx"), lax.axis_size("gz")
    chips, rows = groups_z // 2, low_u.shape[0]
    points = cells_x * cells_z
    modes = groups_x * groups_z * rows
    dma = pltpu.SemaphoreType.DMA
    narrow, wide = jnp.bfloat16, jnp.float32
    gather_sems = [
        dma((groups_x, chips)), dma((chips,)), dma((groups_x, chips)), dma((groups_x, groups_z)),
    ]
    scatter_buffers = [
        pltpu.VMEM((groups_x, chips, 2, rows, levels), wide),
        pltpu.VMEM((groups_x, chips, rows, levels), wide),
        pltpu.VMEM((groups_x, chips, rows, levels), narrow),
        pltpu.VMEM((groups_x, chips, rows, levels), narrow),
        pltpu.VMEM((chips, rows, levels), wide),
        pltpu.VMEM((chips, rows, levels), narrow),
        pltpu.VMEM((chips, rows, levels), narrow),
        [dma((groups_x,))] * 4 + [dma((chips,))] * 2,
    ]
    vmem, hbm = pl.BlockSpec(memory_space=pltpu.VMEM), pl.BlockSpec(memory_space=pltpu.HBM)

    def body(*refs):
        step_kernel(groups_x, groups_z, *refs)

    cross, tables_t, all_cross, answer = pl.pallas_call(
        body,
        out_shape=(
            jax.ShapeDtypeStruct((points, levels), wide),
            jax.ShapeDtypeStruct((points, modes), narrow),
            jax.ShapeDtypeStruct((groups_x, groups_z, rows, levels), narrow),
            jax.ShapeDtypeStruct((rows, levels), wide),
        ),
        in_specs=[hbm] * 7,
        out_specs=(vmem, vmem, vmem, vmem),
        scratch_shapes=[
            pltpu.VMEM(high_u.shape, narrow),
            pltpu.VMEM(high_u.shape, narrow),
            pltpu.VMEM(tau_inverse.shape, narrow),
            pltpu.VMEM((groups_x, groups_z, rows, 2 * levels), narrow),
            pltpu.VMEM((modes, points), narrow),
            pltpu.VMEM((2, points, levels), narrow),
            pltpu.VMEM((2, 1, rows), jnp.int32),
            pltpu.VMEM((groups_x, groups_z, rows, LANES), narrow),
            dma((7,)),
            gather_sems,
            gather_sems,
            gather_sems,
            scatter_buffers,
            scatter_buffers,
        ],
        compiler_params=pltpu.CompilerParams(
            collective_id=0, has_side_effects=True, vmem_limit_bytes=LIMIT_ONE
        ),
        name="step",
    )(
        *(
            pltpu.with_memory_space_constraint(array, pltpu.HBM)
            for array in (
                high_u, high_v, low_u, low_v, low_kx.reshape(1, rows), low_kz.reshape(1, rows),
                tau_inverse,
            )
        )
    )
    unitary = 1.0 / math.sqrt(groups_x * cells_x * groups_z * cells_z)

    def last(*refs):
        finish_kernel(unitary, *refs)

    return pl.pallas_call(
        last,
        out_shape=(
            jax.ShapeDtypeStruct(high_u.shape, narrow),
            jax.ShapeDtypeStruct((rows, levels), wide),
        ),
        in_specs=[vmem, vmem, vmem, vmem],
        out_specs=(hbm, vmem),
        scratch_shapes=[pltpu.VMEM(high_u.shape, narrow), dma((points // row_block(points),))],
        compiler_params=pltpu.CompilerParams(vmem_limit_bytes=LIMIT_TWO),
        name="finish",
    )(cross, tables_t, all_cross, answer)


def solution(mesh):
    placed = (
        P("gx", "gz", None),
        P("gx", "gz", None),
        P(("gx", "gz"), None),
        P(("gx", "gz"), None),
        P(("gx", "gz")),
        P(("gx", "gz")),
        P(("gx", "gz"), None, None),
    )
    return jax.shard_map(
        on_device,
        mesh=mesh,
        in_specs=placed,
        out_specs=(P("gx", "gz", None), P(("gx", "gz"), None)),
        check_vma=False,
    )
```

```python
import math

import jax
import jax.numpy as jnp
from jax import lax
from jax.experimental import pallas as pl
from jax.experimental.pallas import tpu as pltpu
from jax.sharding import PartitionSpec as P

KL = 32
LANES = 128
MESH = pl.DeviceIdType.MESH


NT = (((1,), (1,)), ((), ()))


def wrapped(phase, length):
    return phase & (length - 1) if length & (length - 1) == 0 else lax.rem(phase, length)


def row_block(points):
    return 256 if points % 256 == 0 else points


def copy_to(src, dst, send, recv, device):
    return pltpu.make_async_remote_copy(
        src_ref=src, dst_ref=dst, send_sem=send, recv_sem=recv, device_id=device, device_id_type=MESH
    )


class Place:
    def __init__(self, groups_x, groups_z):
        self.nx, self.nc = groups_x, groups_z // 2
        self.g = lax.axis_index("gx")
        gz = lax.axis_index("gz")
        self.gz = gz
        self.c, self.k = gz // 2, gz % 2

    def partner(self):
        return (self.g, 2 * self.c + 1 - self.k)

    def along_x(self, i):
        return lax.rem(self.g + i, self.nx)

    def along_c(self, j):
        return lax.rem(self.c + j, self.nc)


def greet(p):
    barrier = pltpu.get_barrier_semaphore()
    pl.semaphore_signal(barrier, inc=1, device_id=p.partner(), device_id_type=MESH)

    @pl.loop(1, p.nx)
    def _(i):
        pl.semaphore_signal(barrier, inc=1, device_id=(p.along_x(i), p.gz), device_id_type=MESH)

    @pl.loop(1, p.nc)
    def _(j):
        pl.semaphore_signal(
            barrier, inc=1, device_id=(p.g, 2 * p.along_c(j) + p.k), device_id_type=MESH
        )

    return lambda: pl.semaphore_wait(barrier, 1 + p.nx - 1 + p.nc - 1)


class Gather:
    def __init__(self, p, out, send_x, send_c, send_p, recv):
        self.p, self.out = p, out
        self.send_x, self.send_c, self.send_p, self.recv = send_x, send_c, send_p, recv

    def at(self, g, gz):
        return self.out.at[g, gz]

    def to_x(self, i, c):
        p, gz = self.p, 2 * c + self.p.k
        return copy_to(
            self.at(p.g, gz), self.at(p.g, gz), self.send_x.at[i, c], self.recv.at[p.g, gz],
            (p.along_x(i), p.gz),
        )

    def to_c(self, j):
        p = self.p
        return copy_to(
            self.at(p.g, p.gz), self.at(p.g, p.gz), self.send_c.at[j], self.recv.at[p.g, p.gz],
            (p.g, 2 * p.along_c(j) + p.k),
        )

    def to_p(self, g, c):
        gz = 2 * c + self.p.k
        return copy_to(
            self.at(g, gz), self.at(g, gz), self.send_p.at[g, c], self.recv.at[g, gz],
            self.p.partner(),
        )

    def arrived(self, g, gz):
        copy_to(
            self.at(g, gz), self.at(g, gz), self.send_c.at[0], self.recv.at[g, gz],
            self.p.partner(),
        ).wait_recv()

    def start(self):
        p = self.p

        @pl.loop(1, p.nc)
        def _(j):
            self.to_c(j).start()

        @pl.loop(1, p.nx)
        def _(i):
            self.to_x(i, p.c).start()

        self.to_p(p.g, p.c).start()

    def relay_c(self):
        p = self.p

        @pl.loop(1, p.nc)
        def _(j):
            c = p.along_c(j)
            self.arrived(p.g, 2 * c + p.k)

            @pl.loop(1, p.nx)
            def _(i):
                self.to_x(i, c).start()

            self.to_p(p.g, c).start()

    def relay_x(self):
        p = self.p

        @pl.loop(0, p.nc)
        def _(j):
            c = p.along_c(j)

            @pl.loop(1, p.nx)
            def _(i):
                g = p.along_x(i)
                self.arrived(g, 2 * c + p.k)
                self.to_p(g, c).start()

    def from_partner(self, g):
        p = self.p

        @pl.loop(0, p.nc)
        def _(j):
            self.arrived(g, 2 * p.along_c(j) + 1 - p.k)

    def drain(self):
        p = self.p

        @pl.loop(1, p.nc)
        def _(j):
            self.to_c(j).wait_send()

        @pl.loop(0, p.nc)
        def _(c):
            @pl.loop(1, p.nx)
            def _(i):
                self.to_x(i, c).wait_send()

            @pl.loop(0, p.nx)
            def _(g):
                self.to_p(g, c).wait_send()


class Scatter:
    def __init__(self, p, part, thin, pair, sums, from_x, acc, sent_c, from_c, sems):
        self.p, self.part, self.thin, self.pair = p, part, thin, pair
        self.sums, self.from_x = sums, from_x
        self.acc, self.sent_c, self.from_c = acc, sent_c, from_c
        self.send_p, self.recv_p, self.send_x, self.recv_x, self.send_c, self.recv_c = sems

    def to_p(self, g):
        return copy_to(
            self.thin.at[g, :, 1 - self.p.k], self.pair.at[g], self.send_p.at[g],
            self.recv_p.at[g], self.p.partner(),
        )

    def to_x(self, i):
        p = self.p
        g = p.along_x(i)
        return copy_to(
            self.sums.at[g], self.from_x.at[p.g], self.send_x.at[g], self.recv_x.at[p.g], (g, p.gz)
        )

    def to_c(self, j):
        p = self.p
        c = p.along_c(j)
        return copy_to(
            self.sent_c.at[c], self.from_c.at[p.c], self.send_c.at[c], self.recv_c.at[p.c],
            (p.g, 2 * c + p.k),
        )

    def chip_sum(self, g):
        self.to_p(g).wait_recv()
        return self.part[g, :, self.p.k] + self.pair[g].astype(jnp.float32)

    def across_x(self):
        p = self.p

        @pl.loop(1, p.nx)
        def _(i):
            g = p.along_x(i)
            self.sums[g] = self.chip_sum(g).astype(self.sums.dtype)
            self.to_x(i).start()

        self.acc[...] = self.chip_sum(p.g)

    def across_c(self):
        p = self.p

        @pl.loop(1, p.nx)
        def _(i):
            g = p.along_x(i)
            copy_to(
                self.sums.at[g], self.from_x.at[g], self.send_x.at[g], self.recv_x.at[g], p.partner()
            ).wait_recv()
            self.acc[...] += self.from_x[g].astype(jnp.float32)

        @pl.loop(1, p.nc)
        def _(j):
            c = p.along_c(j)
            self.sent_c[c] = self.acc[c].astype(self.sent_c.dtype)
            self.to_c(j).start()

    def total(self):
        p = self.p

        @pl.loop(1, p.nc)
        def _(j):
            c = p.along_c(j)
            copy_to(
                self.sent_c.at[c], self.from_c.at[c], self.send_c.at[c], self.recv_c.at[c],
                p.partner(),
            ).wait_recv()
            self.acc[p.c] += self.from_c[c].astype(jnp.float32)

        return self.acc[p.c]

    def drain(self):
        p = self.p

        @pl.loop(0, p.nx)
        def _(g):
            self.to_p(g).wait_send()

        @pl.loop(1, p.nx)
        def _(i):
            self.to_x(i).wait_send()

        @pl.loop(1, p.nc)
        def _(j):
            self.to_c(j).wait_send()


LIMIT_ONE = 48 * 1024 * 1024
LIMIT_TWO = 16 * 1024 * 1024


def step_kernel(
    groups_x, groups_z,
    high_u, high_v, low_u, low_v, low_kx, low_kz, tau,
    cross, tables_t, all_cross, answer,
    fine_u, fine_v, inverse, every, tables, products, lines, marks,
    load, ahead_sems, first_sems, second_sems, cross_buffers, self_buffers,
):
    p = Place(groups_x, groups_z)
    all_here = greet(p)
    cells_x, cells_z, levels = fine_u.shape
    points = cells_x * cells_z
    rows = low_u.shape[0]
    group = groups_z * rows
    lengths = (groups_x * cells_x, groups_z * cells_z)
    unitary = 1.0 / math.sqrt(lengths[0] * lengths[1])

    mine = every.at[p.g, p.gz]
    own = [
        pltpu.make_async_copy(low_u, mine.at[:, pl.ds(0, levels)], load.at[0]),
        pltpu.make_async_copy(low_v, mine.at[:, pl.ds(levels, levels)], load.at[1]),
    ]
    fields = [
        pltpu.make_async_copy(high_u, fine_u, load.at[3]),
        pltpu.make_async_copy(high_v, fine_v, load.at[4]),
        pltpu.make_async_copy(tau, inverse, load.at[5]),
    ]
    indices = [
        pltpu.make_async_copy(low_kx, lines.at[0], load.at[2]),
        pltpu.make_async_copy(low_kz, lines.at[1], load.at[6]),
    ]
    for copy in indices + own + fields:
        copy.start()
    slot = lax.broadcasted_iota(jnp.int32, (rows, rows), 0)
    straight = slot == lax.broadcasted_iota(jnp.int32, (rows, rows), 1)

    def upright(line):
        spread = jnp.broadcast_to(line.astype(jnp.float32), (rows, rows))
        return jnp.sum(jnp.where(straight, spread, 0.0), axis=1, keepdims=True)

    for copy in indices:
        copy.wait()
    kx, kz = upright(lines[0]), upright(lines[1])
    weight = jnp.where(kx > 0, 2.0, 1.0) * jnp.where(kz > 0, 2.0, 1.0)
    first_lanes = lax.broadcasted_iota(jnp.int32, (rows, LANES), 1) < cells_x
    marks[p.g, p.gz] = jnp.where(first_lanes, kx, kz).astype(marks.dtype)
    all_here()
    ahead = Gather(p, marks, *ahead_sems)
    ahead.start()
    for copy in own:
        copy.wait()
    first = Gather(p, every, *first_sems)
    first.start()

    lane = lax.broadcasted_iota(jnp.int32, (group, LANES), 1)
    on_x = lane < cells_x
    place = jnp.where(on_x, p.g * cells_x + lane, p.gz * cells_z + lane - cells_x)
    ahead.relay_c()
    first.relay_c()
    ahead.relay_x()

    def build(i, _):
        g = p.along_x(i)
        ahead.from_partner(g)
        index = marks[g].reshape(group, LANES)
        index = index.astype(jnp.float32).astype(jnp.int32)
        even = index <= KL
        phase = jnp.where(even, index, index - KL) * place

        def angle(length):
            shifted = jnp.where(even, phase, phase + (length - length // 4))
            return wrapped(shifted, length).astype(jnp.float32) * (2.0 * math.pi / length)

        table = jnp.cos(jnp.where(on_x, angle(lengths[0]), angle(lengths[1])))
        turned = table.T
        along_z = turned[cells_x : cells_x + cells_z, :]
        at = pl.ds(pl.multiple_of(g * group, LANES), group)
        for x in range(cells_x):
            slab = turned[x : x + 1, :] * along_z
            tables_t[pl.ds(x * cells_z, cells_z), at] = slab.astype(tables_t.dtype)
        return 0

    lax.fori_loop(0, p.nx, build, 0)

    def turn(g, _):
        at = pl.ds(pl.multiple_of(g * group, LANES), group)
        tables[at, :] = tables_t[:, at].T
        return 0

    lax.fori_loop(0, p.nx, turn, 0)
    first.relay_x()

    @pl.loop(0, p.nx)
    def _(g):
        first.from_partner(g)

    fields[0].wait()
    fields[1].wait()
    modes = groups_x * group
    block = row_block(points)
    planes = block // cells_z

    def multiply(b, _):
        at = pl.ds(pl.multiple_of(b * block, block), block)
        held = every[...].reshape(modes, 2 * levels)
        coarse = jnp.dot(tables_t[at, :], held, preferred_element_type=jnp.float32)
        coarse_u, coarse_v = coarse[:, :levels], coarse[:, levels:]
        u = fine_u[pl.ds(b * planes, planes)].reshape(block, levels).astype(jnp.float32)
        v = fine_v[pl.ds(b * planes, planes)].reshape(block, levels).astype(jnp.float32)
        mixed = coarse_u * v + u * coarse_v
        cross[at, :] = mixed
        products[0, at, :] = mixed.astype(products.dtype)
        products[1, at, :] = (coarse_u * coarse_v + u * v).astype(products.dtype)
        return 0

    lax.fori_loop(0, points // block, multiply, 0)

    def project(scatter, which):
        def one(i, _):
            g = p.along_x(i)
            at = pl.ds(pl.multiple_of(g * group, LANES), group)
            value = jnp.dot(
                tables[at, :], products[which], preferred_element_type=jnp.float32
            ).reshape(p.nc, 2, rows, levels)
            scatter.part[g] = value
            if scatter.thin is not scatter.part:
                scatter.thin[g] = value.astype(scatter.thin.dtype)
            scatter.to_p(g).start()
            return 0

        lax.fori_loop(1, p.nx + 1, one, 0)

    crossed = Scatter(p, *cross_buffers)
    selfed = Scatter(p, self_buffers[0], *self_buffers)
    project(crossed, 0)
    crossed.across_x()
    project(selfed, 1)
    selfed.across_x()
    crossed.across_c()
    selfed.across_c()
    all_cross[p.g, p.gz] = (weight * (crossed.total() * unitary)).astype(all_cross.dtype)
    second = Gather(p, all_cross, *second_sems)
    second.start()
    forcing = (selfed.total() * unitary).astype(jnp.bfloat16)
    fields[2].wait()
    row = lax.broadcasted_iota(jnp.int32, (rows, levels), 0)
    answer[...] = jnp.zeros_like(answer)

    def solve(m, _):
        full = lax.dot_general(forcing, inverse[m], NT, preferred_element_type=jnp.float32)
        answer[...] += jnp.where(row == m, full, 0.0)
        return 0

    lax.fori_loop(0, rows // 4, solve, 0)
    second.relay_c()
    lax.fori_loop(rows // 4, rows, solve, 0)
    second.relay_x()

    @pl.loop(0, p.nx)
    def _(g):
        second.from_partner(g)

    ahead.drain()
    first.drain()
    second.drain()
    crossed.drain()
    selfed.drain()


def finish_kernel(unitary, cross, tables_t, all_cross, answer, high_term, response, mirror, sems):
    points, levels = cross.shape
    cells_z = high_term.shape[1]
    block = row_block(points)
    planes = block // cells_z
    modes = tables_t.shape[1]
    response[...] = answer[...]

    def writing(b):
        at = pl.ds(b * planes, planes)
        return pltpu.make_async_copy(mirror.at[at], high_term.at[at], sems.at[b])

    def finish(b, _):
        at = pl.ds(pl.multiple_of(b * block, block), block)
        held = all_cross[...].reshape(modes, levels)
        restored = jnp.dot(tables_t[at, :], held, preferred_element_type=jnp.float32)
        part = (cross[at, :] - unitary * restored).astype(mirror.dtype)
        mirror[pl.ds(b * planes, planes)] = part.reshape(planes, cells_z, levels)
        writing(b).start()
        return 0

    lax.fori_loop(0, points // block, finish, 0)

    @pl.loop(0, points // block)
    def _(b):
        writing(b).wait()


def on_device(high_u, high_v, low_u, low_v, low_kx, low_kz, tau_inverse):
    cells_x, cells_z, levels = high_u.shape
    groups_x, groups_z = lax.axis_size("gx"), lax.axis_size("gz")
    chips, rows = groups_z // 2, low_u.shape[0]
    points = cells_x * cells_z
    modes = groups_x * groups_z * rows
    dma = pltpu.SemaphoreType.DMA
    narrow, wide = jnp.bfloat16, jnp.float32
    gather_sems = [
        dma((groups_x, chips)), dma((chips,)), dma((groups_x, chips)), dma((groups_x, groups_z)),
    ]
    own_part = pltpu.VMEM((groups_x, chips, 2, rows, levels), wide)
    cross_first = [
        own_part,
        pltpu.VMEM((groups_x, chips, 2, rows, levels), narrow),
        pltpu.VMEM((groups_x, chips, rows, levels), narrow),
    ]
    self_first = [own_part, pltpu.VMEM((groups_x, chips, rows, levels), wide)]
    scatter_buffers = [
        pltpu.VMEM((groups_x, chips, rows, levels), narrow),
        pltpu.VMEM((groups_x, chips, rows, levels), narrow),
        pltpu.VMEM((chips, rows, levels), wide),
        pltpu.VMEM((chips, rows, levels), narrow),
        pltpu.VMEM((chips, rows, levels), narrow),
        [dma((groups_x,))] * 4 + [dma((chips,))] * 2,
    ]
    vmem, hbm = pl.BlockSpec(memory_space=pltpu.VMEM), pl.BlockSpec(memory_space=pltpu.HBM)

    def body(*refs):
        step_kernel(groups_x, groups_z, *refs)

    cross, tables_t, all_cross, answer = pl.pallas_call(
        body,
        out_shape=(
            jax.ShapeDtypeStruct((points, levels), wide),
            jax.ShapeDtypeStruct((points, modes), narrow),
            jax.ShapeDtypeStruct((groups_x, groups_z, rows, levels), narrow),
            jax.ShapeDtypeStruct((rows, levels), wide),
        ),
        in_specs=[hbm] * 7,
        out_specs=(vmem, vmem, vmem, vmem),
        scratch_shapes=[
            pltpu.VMEM(high_u.shape, narrow),
            pltpu.VMEM(high_u.shape, narrow),
            pltpu.VMEM(tau_inverse.shape, narrow),
            pltpu.VMEM((groups_x, groups_z, rows, 2 * levels), narrow),
            pltpu.VMEM((modes, points), narrow),
            pltpu.VMEM((2, points, levels), narrow),
            pltpu.VMEM((2, 1, rows), jnp.int32),
            pltpu.VMEM((groups_x, groups_z, rows, LANES), narrow),
            dma((7,)),
            gather_sems,
            gather_sems,
            gather_sems,
            cross_first + scatter_buffers,
            self_first + scatter_buffers,
        ],
        compiler_params=pltpu.CompilerParams(
            collective_id=0, has_side_effects=True, vmem_limit_bytes=LIMIT_ONE
        ),
        name="step",
    )(
        *(
            pltpu.with_memory_space_constraint(array, pltpu.HBM)
            for array in (
                high_u, high_v, low_u, low_v, low_kx.reshape(1, rows), low_kz.reshape(1, rows),
                tau_inverse,
            )
        )
    )
    unitary = 1.0 / math.sqrt(groups_x * cells_x * groups_z * cells_z)

    def last(*refs):
        finish_kernel(unitary, *refs)

    return pl.pallas_call(
        last,
        out_shape=(
            jax.ShapeDtypeStruct(high_u.shape, narrow),
            jax.ShapeDtypeStruct((rows, levels), wide),
        ),
        in_specs=[vmem, vmem, vmem, vmem],
        out_specs=(hbm, vmem),
        scratch_shapes=[pltpu.VMEM(high_u.shape, narrow), dma((points // row_block(points),))],
        compiler_params=pltpu.CompilerParams(vmem_limit_bytes=LIMIT_TWO),
        name="finish",
    )(cross, tables_t, all_cross, answer)


def solution(mesh):
    placed = (
        P("gx", "gz", None),
        P("gx", "gz", None),
        P(("gx", "gz"), None),
        P(("gx", "gz"), None),
        P(("gx", "gz")),
        P(("gx", "gz")),
        P(("gx", "gz"), None, None),
    )
    return jax.shard_map(
        on_device,
        mesh=mesh,
        in_specs=placed,
        out_specs=(P("gx", "gz", None), P(("gx", "gz"), None)),
        check_vma=False,
    )
```
